512 devices in a mesh: ctx: 32 (over x, z_hi, core), tp: 16 (over y, z_lo).
Axes of the slice: x: 4, y: 8, z: 8 (z_hi: 4, z_lo: 2; z = z_hi * 2 + z_lo), core: 2. Of those that a mesh axis runs over, the one named last changes fastest.
Arguments:
- queries: bfloat16 [8192, 2048], P('ctx', 'tp'), may hold values from -24 to 24
- key_heads: bfloat16 [8192, 4, 128], P('ctx'), may hold values from -6 to 6
- head_values: bfloat16 [8192, 4, 128], P('ctx'), may hold values from -6 to 6
- hidden: bfloat16 [8192, 4096], P('ctx'), may hold values from -0.59765625 to 0.59765625
- out_proj: bfloat16 [2048, 4096], P('tp'), may hold values from -0.125 to 0.125
- norm_gain: float32 [4096], replicated, may hold values from 0.25 to 1.75
- x_proj: bfloat16 [4096, 4096], P('ctx', 'tp'), may hold values from -0.046875 to 0.046875
- bc_proj: bfloat16 [4096, 4, 256], P('ctx'), may hold values from -0.09375 to 0.09375
- dt_proj: bfloat16 [4096, 64], P('ctx', 'tp'), may hold values from -0.09375 to 0.09375
- dt_bias: float32 [64], P('tp'), may hold values from -12 to 0
- decay_log: float32 [64], P('tp'), may hold values from -10 to 3
- skip_gain: float32 [64], P('tp'), may hold values from 0.5 to 1.5
Outputs:
- residual_out: bfloat16 [8192, 4096], P('ctx', 'tp')
- mamba_out: bfloat16 [8192, 4096], P('ctx', 'tp')
The draws below stay inside these ranges and needn't reach their ends.
All inputs are finite; a program needn't handle non-finite values.
Results may differ from the reference program's by a relative error of at most 0.034.
Values may be sent and summed in bfloat16 or wider, within the bound.
No kernel may reach another device: no remote copies, remote signals or barrier semaphores. Data moves between devices by JAX's collectives and lax.ppermute only.
A program may use at most 64 MiB of HBM per device.

```python
import math
import jax
import jax.numpy as jnp
from jax import lax

D = 4096
HQ = 16
KEY_VALUE_HEADS = 4
HEAD_SIZE = 128
MH = 64
P_SIZE = 64
N = 128
NG = 4
TOK_DEV = 256
TOKEN_COUNT = 8192
BLOCK = 128
GROUP = 4
HPG = 16
N_CTX = 32
N_TP = 16


def query_key_pair(key):
    base_key = jax.random.fold_in(key, 17)
    key_query, random_key_split = jax.random.split(base_key, 2)
    query_vals = jnp.clip(jax.random.normal(key_query, (TOKEN_COUNT, HQ * HEAD_SIZE), jnp.float32), -6.0, 6.0)
    random_key_values = jnp.clip(jax.random.normal(random_key_split, (TOKEN_COUNT, KEY_VALUE_HEADS, HEAD_SIZE), jnp.float32), -6.0, 6.0)
    return (query_vals, random_key_values)


def draw_queries(key, part):
    return query_key_pair(key)[0].astype(jnp.bfloat16)


def draw_key_heads(key, part):
    return query_key_pair(key)[1].astype(jnp.bfloat16)


def decay_pair(key):
    base_key = jax.random.fold_in(key, 29)
    key_kind, key_slow, key_fast, key_jitter = jax.random.split(base_key, 4)
    share = 5
    slow_heads = jax.random.randint(key_kind, (MH,), 0, 10) < share
    slow_rate = jax.random.uniform(key_slow, (MH,), jnp.float32, 0.2, 1.0) / TOKEN_COUNT
    fast_rate = jnp.exp(jax.random.uniform(key_fast, (MH,), jnp.float32, math.log(1.0 / 50.0), math.log(1.0 / 30.0)))
    rate = jnp.where(slow_heads, slow_rate, fast_rate)
    span = jnp.minimum(TOKEN_COUNT * 1.0, 1.0 / rate)
    step_size = jax.random.uniform(key_jitter, (MH,), jnp.float32, 0.7, 1.4) / (11.0 * jnp.sqrt(span))
    bias = jnp.log(jnp.expm1(step_size))
    log_rate = jnp.log(rate / step_size)
    return (bias, log_rate)


def draw_dt_bias(key, part):
    return decay_pair(key)[0]


def draw_decay_log(key, part):
    return decay_pair(key)[1]


def block_scale(stream_key, dims, shards, low, largest):
    def one(axis_at, parts):
        draws = jax.random.uniform(jax.random.fold_in(jax.random.fold_in(stream_key, 6), axis_at), (parts,), jnp.float32, low / len(shards), largest / len(shards))
        return jnp.repeat(jnp.exp(draws), dims[axis_at] // parts).reshape((-1,) + (1,) * (len(dims) - axis_at - 1))

    loudness = one(*shards[0])
    for cut in shards[1:]:
        loudness = loudness * one(*cut)
    return loudness


def bell_draw(stream_key, shape, spread, limit, cuts=(), kind=jnp.bfloat16):
    values = spread * jax.random.normal(stream_key, shape, jnp.float32)
    if cuts:
        values = values * block_scale(stream_key, shape, cuts, -0.22, 0.18)
    return jnp.clip(values, -limit, limit).astype(kind)


def setup_inputs(seed: int = 0) -> dict:
    seeds = jax.random.split(jax.random.key(seed), 13)
    return {
        "queries": draw_queries(jax.random.fold_in(seeds[12], 71), 0),
        "key_heads": draw_key_heads(jax.random.fold_in(seeds[12], 71), 0),
        "head_values": bell_draw(seeds[2], (TOKEN_COUNT, KEY_VALUE_HEADS, HEAD_SIZE), 1.0, 6.0, ((0, 32),)),
        "hidden": bell_draw(seeds[3], (TOKEN_COUNT, D), 0.1, 0.59765625, ((0, 32),)),
        "out_proj": bell_draw(seeds[4], (HQ * HEAD_SIZE, D), (HQ * HEAD_SIZE) ** -0.5, 0.125, ((0, 16),)),
        "norm_gain": jnp.clip(1.0 + 0.15 * jax.random.normal(seeds[5], (D,), jnp.float32), 0.25, 1.75),
        "x_proj": bell_draw(seeds[6], (D, MH * P_SIZE), (4 * D) ** -0.5, 0.046875, ((0, 32), (1, 16))),
        "bc_proj": bell_draw(seeds[7], (D, NG, 2 * N), D ** -0.5, 0.09375, ((0, 32),)),
        "dt_proj": bell_draw(seeds[8], (D, MH), D ** -0.5, 0.09375, ((0, 32), (1, 16))),
        "dt_bias": draw_dt_bias(jax.random.fold_in(seeds[12], 71), 0),
        "decay_log": draw_decay_log(jax.random.fold_in(seeds[12], 71), 0),
        "skip_gain": jnp.clip(0.5 + 1.0 * jax.random.uniform(seeds[11], (MH,), jnp.float32) ** block_scale(seeds[11], (MH,), ((0, 16),), -0.2, 0.2), 0.5, 1.5),
    }


def sequence_rows():
    position = jnp.arange(TOKEN_COUNT, dtype=jnp.int32)
    block = position // BLOCK
    offset = position % BLOCK
    device = jnp.where(block < N_CTX, block, 2 * N_CTX - 1 - block)
    within = jnp.where(block < N_CTX, offset, BLOCK + offset)
    return (device * TOK_DEV + within).astype(jnp.int32)

def row_positions():
    rows = jnp.arange(TOKEN_COUNT, dtype=jnp.int32)
    device = rows // TOK_DEV
    within = rows % TOK_DEV
    block = jnp.where(within < BLOCK, device, 2 * N_CTX - 1 - device)
    return (block * BLOCK + within % BLOCK).astype(jnp.int32)

def reference(queries, key_heads, head_values, hidden, out_proj, norm_gain, x_proj, bc_proj, dt_proj, dt_bias, decay_log, skip_gain):
    order = sequence_rows()
    back = row_positions()
    seq_q = queries[order].reshape(TOKEN_COUNT, HQ, HEAD_SIZE).astype(jnp.float32)
    seq_k = jnp.repeat(key_heads[order].astype(jnp.float32), GROUP, axis=1)
    seq_v = jnp.repeat(head_values[order].astype(jnp.float32), GROUP, axis=1)
    q_block = math.gcd(512, TOKEN_COUNT)
    key_pos = jnp.arange(TOKEN_COUNT, dtype=jnp.int32)

    def attend_block(index):
        start = index * q_block
        part_q = lax.dynamic_slice_in_dim(seq_q, start, q_block, 0)
        scores = jnp.einsum('qhd,khd->hqk', part_q, seq_k, precision=lax.Precision.HIGHEST) / math.sqrt(HEAD_SIZE)
        query_pos = start + jnp.arange(q_block, dtype=jnp.int32)
        allowed = (key_pos[None, :] <= query_pos[:, None])[None]
        top = lax.optimization_barrier(jnp.max(jnp.where(allowed, scores, -1e+30), axis=-1))
        weights = jnp.where(allowed, jnp.exp(scores - top[..., None]), 0.0)
        total = lax.optimization_barrier(jnp.sum(weights, axis=-1))
        rounded = lax.optimization_barrier(weights.astype(jnp.bfloat16)).astype(jnp.float32)
        mixed = jnp.einsum('hqk,khd->qhd', rounded, seq_v, precision=lax.Precision.HIGHEST)
        return (mixed / jnp.transpose(total)[:, :, None]).astype(jnp.bfloat16)
    attended = lax.map(attend_block, jnp.arange(TOKEN_COUNT // q_block, dtype=jnp.int32)).reshape(TOKEN_COUNT, HQ * HEAD_SIZE)
    head_cols = HQ * HEAD_SIZE // N_TP
    grouped_o = jnp.transpose(attended.reshape(TOKEN_COUNT, N_TP, head_cols), (1, 0, 2))
    grouped_w = out_proj.reshape(N_TP, head_cols, D)

    def add_group(running, pair):
        part = jnp.dot(pair[0], pair[1], preferred_element_type=jnp.float32)
        part = lax.optimization_barrier(part.astype(jnp.bfloat16)).astype(jnp.float32)
        return (running + part, None)
    attention_sum, _ = lax.scan(add_group, jnp.zeros((TOKEN_COUNT, D), jnp.float32), (grouped_o, grouped_w))
    residual = (hidden[order].astype(jnp.float32) + attention_sum).astype(jnp.bfloat16)
    as_float = residual.astype(jnp.float32)
    mean_square = lax.optimization_barrier(jnp.mean(as_float * as_float, axis=-1, keepdims=True))
    normed = (as_float * lax.rsqrt(mean_square + 1e-05) * norm_gain).astype(jnp.bfloat16)
    x_seq = lax.optimization_barrier(jnp.dot(normed, x_proj, preferred_element_type=jnp.float32).astype(jnp.bfloat16))
    bc_seq = lax.optimization_barrier(jnp.dot(normed, bc_proj.reshape(D, NG * 2 * N), preferred_element_type=jnp.float32).astype(jnp.bfloat16))
    bc_seq = bc_seq.astype(jnp.float32).reshape(TOKEN_COUNT, NG, 2 * N)
    step_sizes = jax.nn.softplus(jnp.dot(normed, dt_proj, preferred_element_type=jnp.float32) + dt_bias)
    rates = -jnp.exp(decay_log)
    inputs = x_seq.astype(jnp.float32).reshape(TOKEN_COUNT, MH, P_SIZE)

    def advance(state, items):
        x_now, b_now, c_now, step_now = items
        b_rows = jnp.repeat(b_now, HPG, axis=0)
        c_rows = jnp.repeat(c_now, HPG, axis=0)
        decay = jnp.exp(step_now * rates)
        state = decay[:, None, None] * state + (step_now[:, None] * x_now)[:, :, None] * b_rows[:, None, :]
        output = jnp.einsum('hpn,hn->hp', state, c_rows, precision=lax.Precision.HIGHEST) + skip_gain[:, None] * x_now
        return (state, output)
    _, outputs = lax.scan(advance, jnp.zeros((MH, P_SIZE, N), jnp.float32), (inputs, bc_seq[..., :N], bc_seq[..., N:], step_sizes))
    mamba = outputs.reshape(TOKEN_COUNT, MH * P_SIZE).astype(jnp.bfloat16)
    return (residual[back], mamba[back])
```

```python
import math

import jax
import jax.numpy as jnp
from jax import lax
from jax.sharding import Mesh
from jax.sharding import PartitionSpec as P

AXES = ("x", "zhh", "zhl", "co", "yhi", "ylo", "zl")
SIZES = (4, 2, 2, 2, 4, 2, 2)
ZH = ("zhh", "zhl")
CTX = ("x", "zhh", "zhl", "co")
Y = ("yhi", "ylo")
TP = ("yhi", "ylo", "zl")
BF = jnp.bfloat16
F32 = jnp.float32
LOWEST = -1e30


def split3(value):
    first = value.astype(BF)
    rest = value - first.astype(F32)
    second = rest.astype(BF)
    third = (rest - second.astype(F32)).astype(BF)
    return first, second, third


def swap(value, axis):
    return lax.ppermute(value, axis, [(0, 1), (1, 0)])


def exchange(value, axes):
    return lax.all_to_all(value, axes, split_axis=0, concat_axis=0, tiled=True)


def split_product(form, wide, narrow):
    upper = wide.astype(BF)
    lower = (wide - upper.astype(F32)).astype(BF)
    first_term = jnp.einsum(form, upper, narrow, preferred_element_type=F32)
    return first_term + jnp.einsum(form, lower, narrow, preferred_element_type=F32)


def body(
    queries,
    key_heads,
    head_values,
    hidden,
    out_proj,
    norm_gain,
    x_proj,
    bc_proj,
    dt_proj,
    dt_bias,
    decay_log,
    skip_gain,
):
    ctx = lax.axis_index(CTX)
    group = lax.axis_index("yhi")
    ylo = lax.axis_index("ylo")
    zl = lax.axis_index("zl")
    y = lax.axis_index(Y)
    quarter = 2 * ylo + zl

    bc_half = lax.dynamic_slice(bc_proj, (0, group, 128 * zl), (128, 1, 128))[:, 0]
    packed = jnp.concatenate(
        [x_proj, bc_half, jnp.pad(dt_proj, ((0, 0), (0, 124)))], axis=1
    )
    packed = lax.ppermute(packed, ("zhl", "zl"), [(0, 0), (1, 2), (2, 1), (3, 3)])
    weights = lax.all_gather(packed, ("zhl", "x", "zhh", "co"), axis=0, tiled=True)
    weights = weights.reshape(2, 2048, 512)

    other_q = swap(queries, "zl")
    pair_q = jnp.where(
        zl == 0, jnp.stack([queries, other_q]), jnp.stack([other_q, queries])
    )
    other_q = swap(pair_q, "ylo")
    four_q = jnp.where(
        ylo == 0,
        jnp.concatenate([pair_q, other_q]),
        jnp.concatenate([other_q, pair_q]),
    )

    by_zl = out_proj.reshape(128, 8, 2, 256)
    mine = lax.dynamic_index_in_dim(by_zl, zl, 2, keepdims=False)
    theirs = lax.dynamic_index_in_dim(by_zl, 1 - zl, 2, keepdims=False)
    pair_w = jnp.stack([mine, swap(theirs, "zl")]).reshape(2, 128, 2048)
    four_w = jnp.concatenate([pair_w, swap(pair_w, "ylo")])

    def part(heads):
        return lax.dynamic_slice(
            heads.reshape(2, 128, 4, 128), (0, 32 * quarter, group, 0), (2, 32, 1, 128)
        ).reshape(1, 64, 128)

    both = jnp.concatenate([part(key_heads), part(head_values)])[None]
    both = lax.all_gather(both, ZH, axis=0, tiled=True)
    both = lax.all_gather(both, "x", axis=0, tiled=True)
    keys = lax.all_gather(both[:, 0], "co", axis=0, tiled=True).reshape(2048, 128)
    values = lax.all_gather(both[:, 1], "co", axis=0, tiled=True).reshape(2048, 128)

    spot = jnp.arange(2048, dtype=jnp.int32)
    source = (spot // 64 % 16) * 2 + spot // 1024
    block = jnp.where(spot % 64 < 32, source, 63 - source)
    key_pos = block * 128 + 32 * quarter + spot % 32
    row = jnp.arange(256, dtype=jnp.int32)
    query_pos = jnp.where(row < 128, ctx, 63 - ctx) * 128 + row % 128
    scores = jnp.einsum(
        "hqd,kd->hqk", four_q, keys, preferred_element_type=F32
    ) / math.sqrt(128)
    allowed = key_pos[None, :] <= query_pos[:, None]
    top = jnp.max(jnp.where(allowed, scores, LOWEST), axis=-1)
    raised = jnp.where(allowed, jnp.exp(scores - top[..., None]), 0.0)
    total = jnp.sum(raised, axis=-1)
    summed = jnp.einsum("hqk,kd->hqd", raised.astype(BF), values, preferred_element_type=F32)
    safe = jnp.where(total > 0, total, 1.0)
    share = (summed / safe[..., None]).astype(BF)
    level = jnp.where(total > 0, top + jnp.log(safe), LOWEST)

    share = jnp.transpose(share.reshape(4, 4, 2, 32, 128), (2, 0, 1, 3, 4)).reshape(2, 512, 128)
    level = jnp.transpose(level.reshape(4, 4, 2, 32), (2, 0, 1, 3)).reshape(2, 4, 128)
    sent = jnp.concatenate([share, *split3(level), jnp.zeros((2, 4, 128), BF)], axis=1)
    sent = jnp.broadcast_to(sent[:, None], (2, 2, 528, 128)).reshape(4 * 528, 128)
    came = exchange(sent, ("ylo", "zl")).reshape(4, 528, 128)
    levels = came[:, 512:524].reshape(4, 3, 512).astype(F32)
    levels = (levels[:, 2] + levels[:, 1]) + levels[:, 0]
    scale = jnp.exp(levels - jnp.max(levels, axis=0))
    scale = scale / jnp.sum(scale, axis=0)
    attended = jnp.sum(scale[..., None] * came[:, :512].astype(F32), axis=0).astype(BF)
    attended = attended.reshape(4, 128, 128)
    relative = jnp.stack(
        [lax.dynamic_index_in_dim(attended, quarter ^ r, 0, keepdims=False) for r in range(4)]
    )
    head_part = jnp.einsum("rtd,rdn->tn", relative, four_w, preferred_element_type=F32)

    parts = exchange(head_part.astype(BF), "yhi").reshape(4, 32, 2048)
    attention_sum = jnp.sum(parts.astype(F32), axis=0)
    hidden_mine = lax.dynamic_slice(
        hidden.reshape(256, 8, 2, 256), (32 * y, 0, zl, 0), (32, 8, 1, 256)
    ).reshape(32, 2048)
    residual = (hidden_mine.astype(F32) + attention_sum).astype(BF)
    spread = jnp.broadcast_to(residual[None], (8, 32, 2048)).reshape(256, 2048)
    residual = exchange(spread, Y)
    residual_out = lax.dynamic_slice(residual, (0, 256 * y), (256, 256))

    gain = lax.dynamic_index_in_dim(norm_gain.reshape(8, 2, 256), zl, 1, keepdims=False)
    as_float = residual.astype(F32)
    square = jnp.sum(as_float * as_float, axis=-1, keepdims=True)
    gained = (as_float * gain.reshape(1, 2048)).astype(BF)
    sums = jnp.einsum("tk,zkn->ztn", gained, weights, preferred_element_type=F32)
    own = lax.dynamic_index_in_dim(sums, zl, 0, keepdims=False)
    away = lax.dynamic_index_in_dim(sums, 1 - zl, 0, keepdims=False)
    sum_bc = jnp.concatenate([sums[0, :, 256:384], sums[1, :, 256:384]], axis=1)
    fine = jnp.concatenate(split3(jnp.concatenate([away[:, 384:388], square], axis=1)), axis=1)
    sent = jnp.concatenate(
        [away[:, :256].astype(BF), sum_bc.astype(BF), jnp.pad(fine, ((0, 0), (0, 113)))], axis=1
    )
    came = swap(sent, "zl").astype(F32)
    fine = came[:, 512:527].reshape(256, 3, 5)
    fine = (fine[:, 2] + fine[:, 1]) + fine[:, 0]
    norm = lax.rsqrt((square + fine[:, 4:5]) / 4096.0 + 1e-05)
    sum_x = (own[:, :256] + came[:, :256]) * norm
    sum_bc = (sum_bc + came[:, 256:512]) * norm
    sum_dt = (own[:, 384:388] + fine[:, :4]) * norm

    half = 128
    inputs_low = sum_x.astype(BF).reshape(2, half, 1, 4, 64)
    inputs = inputs_low.astype(F32)
    bc_round = sum_bc.astype(BF).reshape(2, half, 1, 256)
    b_low = bc_round[..., :128]
    c_low = bc_round[..., 128:]
    steps = jax.nn.softplus(sum_dt + dt_bias).reshape(2, half, 1, 4)
    rates = -jnp.exp(decay_log).reshape(1, 4)
    cumul = jnp.transpose(jnp.cumsum(steps * rates, axis=1), (0, 2, 3, 1))
    step_rows = jnp.transpose(steps, (0, 2, 3, 1))
    gram = jnp.einsum("ckgn,csgn->cgks", c_low, b_low, preferred_element_type=F32)
    places = jnp.arange(half, dtype=jnp.int32)
    causal = places[None, :] <= places[:, None]
    gaps = cumul[..., :, None] - cumul[..., None, :]
    decay = jnp.where(causal, jnp.exp(jnp.where(causal, gaps, 0.0)), 0.0)
    mixing = gram[:, :, None] * decay * step_rows[..., None, :]
    inner = split_product("cgjks,csgjp->ckgjp", mixing, inputs_low)
    last = cumul[..., -1]
    tail = jnp.exp(last[..., None] - cumul) * step_rows
    weighted = jnp.transpose(tail, (0, 3, 1, 2))[..., None] * inputs
    block_state = split_product("csgjp,csgn->cgjpn", weighted, b_low)
    block_decay = jnp.exp(last)

    rows = jnp.transpose(block_state.reshape(2, 32, 8, 128), (1, 0, 2, 3)).reshape(32, 16, 128)
    decays = jnp.repeat(block_decay.reshape(2, 4).T, 8, axis=0)
    decays = jnp.broadcast_to(decays[..., None], (32, 2, 128))
    sent = jnp.concatenate([rows, decays, jnp.zeros((32, 6, 128), F32)], axis=1)
    came = exchange(sent, CTX)
    state = jnp.zeros((8, 128), F32)
    first, second = [], []
    for i in range(32):
        first.append(state)
        state = came[i, 16:17] * state + came[i, :8]
    for i in range(31, -1, -1):
        second.append(state)
        state = came[i, 17:18] * state + came[i, 8:16]
    entering = jnp.stack(
        [jnp.concatenate([a, b]) for a, b in zip(first, second[::-1])]
    )
    entering = exchange(entering, CTX)
    entering = jnp.transpose(entering.reshape(32, 2, 8, 128), (1, 0, 2, 3)).reshape(2, 1, 4, 64, 128)

    carried = jnp.transpose(jnp.exp(cumul), (0, 3, 1, 2))[..., None] * split_product(
        "cgjpn,ckgn->ckgjp", entering, c_low
    )
    output = inner + carried + skip_gain.reshape(1, 4)[:, :, None] * inputs
    mamba_out = output.reshape(256, 256).astype(BF)
    return (residual_out, mamba_out)


def solution(mesh):
    fine = Mesh(mesh.devices.reshape(SIZES), AXES)
    placed = (
        P(CTX, TP),
        P(CTX, None, None),
        P(CTX, None, None),
        P(CTX, None),
        P(TP, None),
        P(),
        P(CTX, TP),
        P(CTX, None, None),
        P(CTX, TP),
        P(TP),
        P(TP),
        P(TP),
    )
    return jax.shard_map(
        body,
        mesh=fine,
        in_specs=placed,
        out_specs=(P(CTX, TP), P(CTX, TP)),
        check_vma=False,
    )
```

```python
import math

import jax
import jax.numpy as jnp
from jax import lax
from jax.experimental import pallas as pl
from jax.experimental.pallas import tpu as pltpu
from jax.sharding import Mesh
from jax.sharding import PartitionSpec as P

AXES = ("x", "zhh", "zhl", "co", "yhi", "ylo", "zl")
SIZES = (4, 2, 2, 2, 4, 2, 2)
ZH = ("zhh", "zhl")
CTX = ("x", "zhh", "zhl", "co")
Y = ("yhi", "ylo")
TP = ("yhi", "ylo", "zl")
BF = jnp.bfloat16
F32 = jnp.float32
LOWEST = -1e30


def split3(value):
    first = value.astype(BF)
    rest = value - first.astype(F32)
    second = rest.astype(BF)
    third = (rest - second.astype(F32)).astype(BF)
    return first, second, third


def features(value, zl):
    return jnp.concatenate(
        [
            lax.dynamic_slice_in_dim(value, 512 * i + 256 * zl, 256, 1)
            for i in range(8)
        ],
        axis=1,
    )


def swap(value, axis):
    return lax.ppermute(value, axis, [(0, 1), (1, 0)])


def exchange(value, axes):
    return lax.all_to_all(value, axes, split_axis=0, concat_axis=0, tiled=True)


def split_product(form, wide, narrow):
    upper = wide.astype(BF)
    lower = (wide - upper.astype(F32)).astype(BF)
    first_term = jnp.einsum(form, upper, narrow, preferred_element_type=F32)
    return first_term + jnp.einsum(form, lower, narrow, preferred_element_type=F32)


def attend(spots, q_ref, k_ref, v_ref, out_ref):
    ctx, quarter = spots[0], spots[1]
    lane = lax.broadcasted_iota(jnp.int32, (32, 256), 1)
    token = lane % 128 // 32 * 64 + lane // 128 * 32 + lane % 32
    seat = jnp.where(token < 128, ctx, 63 - ctx) * 128 + token % 128
    reach = seat - lax.broadcasted_iota(jnp.int32, (32, 256), 0)
    levels = []
    for head in range(4):
        tiles = []
        for chunk in range(8):
            scores = lax.dot_general(
                k_ref[256 * chunk : 256 * (chunk + 1)],
                q_ref[head],
                (((1,), (1,)), ((), ())),
                preferred_element_type=F32,
            ) * (math.log2(math.e) / math.sqrt(128))
            for piece in range(8):
                place = 4 * chunk + piece // 2
                source = place % 16 * 2 + place // 16
                block = source if piece % 2 == 0 else 63 - source
                allowed = reach >= block * 128 + 32 * quarter
                tiles.append(
                    jnp.where(allowed, scores[32 * piece : 32 * (piece + 1)], LOWEST)
                )
        top = tiles[0]
        for tile in tiles[1:]:
            top = jnp.maximum(top, tile)
        top = jnp.max(top, axis=0, keepdims=True)
        total = jnp.zeros((32, 256), F32)
        summed = jnp.zeros((128, 256), F32)
        for chunk in range(8):
            raised = [jnp.exp2(tile - top) for tile in tiles[8 * chunk : 8 * chunk + 8]]
            for part in raised:
                total = total + part
            summed = summed + lax.dot_general(
                v_ref[256 * chunk : 256 * (chunk + 1)],
                jnp.concatenate(raised).astype(BF),
                (((0,), (0,)), ((), ())),
                preferred_element_type=F32,
            )
        total = jnp.sum(total, axis=0, keepdims=True)
        share = (summed / total).astype(BF)
        for dest in range(4):
            half = dest // 2
            out_ref[dest, 128 * head : 128 * (head + 1)] = share[:, 128 * half : 128 * half + 128]
        levels.append(jnp.where(top > 0.5 * LOWEST, top + jnp.log2(total), LOWEST))
    level = jnp.concatenate(levels)
    fine = jnp.concatenate([*split3(level), jnp.zeros((4, 256), BF)])
    for dest in range(4):
        half = dest // 2
        out_ref[dest, 512:528] = fine[:, 128 * half : 128 * half + 128]


def project(spots, came_ref, own_ref, far_ref, out_ref, attended):
    quarter = spots[1]
    fine = [came_ref[source, 512:528].astype(F32) for source in range(4)]
    levels = [(part[8:12] + part[4:8]) + part[0:4] for part in fine]
    top = jnp.maximum(jnp.maximum(levels[0], levels[1]), jnp.maximum(levels[2], levels[3]))
    scales = [jnp.exp2(level - top) for level in levels]
    total = (scales[0] + scales[1]) + (scales[2] + scales[3])
    scales = [scale / total for scale in scales]
    for head in range(4):
        joined = jnp.zeros((128, 128), F32)
        for source in range(4):
            joined = joined + scales[source][head : head + 1] * came_ref[
                source, 128 * head : 128 * (head + 1)
            ].astype(F32)
        attended[head] = joined.astype(BF)
    total = None
    for far, w_ref in ((0, own_ref), (2, far_ref)):
        pair = jnp.concatenate([attended[quarter ^ far], attended[quarter ^ far ^ 1]])
        product = lax.dot_general(
            pair, w_ref[...], (((0,), (0,)), ((), ())), preferred_element_type=F32
        )
        total = product if total is None else total + product
    out_ref[...] = total.astype(BF)


def scan(came_ref, out_ref):
    state = jnp.zeros((8, 128), F32)
    for i in range(32):
        out_ref[i, :8] = state
        state = came_ref[i, 16:17] * state + came_ref[i, :8]
    for i in range(31, -1, -1):
        out_ref[i, 8:] = state
        state = came_ref[i, 17:18] * state + came_ref[i, 8:16]


VM = pl.BlockSpec(memory_space=pltpu.VMEM)
SM = pl.BlockSpec(memory_space=pltpu.SMEM)


def body(
    queries,
    key_heads,
    head_values,
    hidden,
    out_proj,
    norm_gain,
    x_proj,
    bc_proj,
    dt_proj,
    dt_bias,
    decay_log,
    skip_gain,
):
    ctx = lax.axis_index(CTX)
    group = lax.axis_index("yhi")
    ylo = lax.axis_index("ylo")
    zl = lax.axis_index("zl")
    y = lax.axis_index(Y)
    quarter = 2 * ylo + zl

    bc_half = lax.dynamic_slice(bc_proj, (0, group, 128 * zl), (128, 1, 128))[:, 0]
    packed = jnp.concatenate(
        [x_proj, bc_half, jnp.pad(dt_proj, ((0, 0), (0, 124)))], axis=1
    )
    packed = lax.ppermute(packed, ("zhl", "zl"), [(0, 0), (1, 2), (2, 1), (3, 3)])
    weights = lax.all_gather(packed, ("zhl", "x", "zhh", "co"), axis=0, tiled=True)
    weights = weights.reshape(2, 2048, 512)

    spots = jnp.stack([ctx, quarter]).astype(jnp.int32)

    sorted_q = jnp.swapaxes(queries.reshape(4, 2, 32, 128), 0, 1).reshape(256, 128)
    mine = features(out_proj, zl)
    theirs = features(out_proj, 1 - zl)

    def part(heads):
        return lax.dynamic_slice(
            heads.reshape(2, 128, 4, 128), (0, 32 * quarter, group, 0), (2, 32, 1, 128)
        ).reshape(1, 64, 128)

    both = jnp.concatenate([part(key_heads), part(head_values)])[None]
    other_q = swap(sorted_q, "zl")
    other_w = swap(theirs, "zl")
    both = lax.all_gather(both, ZH, axis=0, tiled=True)
    both, other_q, other_w = lax.optimization_barrier((both, other_q, other_w))
    pair_q = jnp.where(
        zl == 0, jnp.stack([sorted_q, other_q]), jnp.stack([other_q, sorted_q])
    )
    pair_w = jnp.concatenate([mine, other_w])
    far_q = swap(pair_q, "ylo")
    far_w = swap(pair_w, "ylo")
    both = lax.all_gather(both, "x", axis=0, tiled=True)
    keys = lax.all_gather(both[:, 0], "co", axis=0, tiled=True).reshape(2048, 128)
    values = lax.all_gather(both[:, 1], "co", axis=0, tiled=True).reshape(2048, 128)
    four_q = jnp.where(
        ylo == 0,
        jnp.concatenate([pair_q, far_q]),
        jnp.concatenate([far_q, pair_q]),
    )

    sent = pl.pallas_call(
        attend,
        out_shape=jax.ShapeDtypeStruct((4, 528, 128), BF),
        in_specs=[SM, VM, VM, VM],
        out_specs=VM,
        compiler_params=pltpu.CompilerParams(vmem_limit_bytes=32 << 20),
        name="attend",
    )(spots, four_q, keys, values)
    came = exchange(sent.reshape(4 * 528, 128), ("ylo", "zl")).reshape(4, 528, 128)
    head_part = pl.pallas_call(
        project,
        out_shape=jax.ShapeDtypeStruct((128, 2048), BF),
        in_specs=[SM, VM, VM, VM],
        out_specs=VM,
        scratch_shapes=[pltpu.VMEM((4, 128, 128), BF)],
        compiler_params=pltpu.CompilerParams(vmem_limit_bytes=32 << 20),
        name="project",
    )(spots, came, pair_w, far_w)

    parts = exchange(head_part, "yhi").reshape(4, 32, 2048)
    attention_sum = jnp.sum(parts.astype(F32), axis=0)
    hidden_mine = features(lax.dynamic_slice(hidden, (32 * y, 0), (32, 4096)), zl)
    residual = (hidden_mine.astype(F32) + attention_sum).astype(BF)
    spread = jnp.broadcast_to(residual[None], (8, 32, 2048)).reshape(256, 2048)
    residual = exchange(spread, Y)
    residual_out = lax.dynamic_slice(residual, (0, 256 * y), (256, 256))

    gain = lax.dynamic_index_in_dim(norm_gain.reshape(8, 2, 256), zl, 1, keepdims=False)
    as_float = residual.astype(F32)
    square = jnp.sum(as_float * as_float, axis=-1, keepdims=True)
    gained = (as_float * gain.reshape(1, 2048)).astype(BF)
    sums = jnp.einsum("tk,zkn->ztn", gained, weights, preferred_element_type=F32)
    own = lax.dynamic_index_in_dim(sums, zl, 0, keepdims=False)
    away = lax.dynamic_index_in_dim(sums, 1 - zl, 0, keepdims=False)
    sum_bc = jnp.concatenate([sums[0, :, 256:384], sums[1, :, 256:384]], axis=1)
    fine = jnp.concatenate(split3(jnp.concatenate([away[:, 384:388], square], axis=1)), axis=1)
    sent = jnp.concatenate(
        [away[:, :256].astype(BF), sum_bc.astype(BF), jnp.pad(fine, ((0, 0), (0, 113)))], axis=1
    )
    came = swap(sent, "zl").astype(F32)
    fine = came[:, 512:527].reshape(256, 3, 5)
    fine = (fine[:, 2] + fine[:, 1]) + fine[:, 0]
    norm = lax.rsqrt((square + fine[:, 4:5]) / 4096.0 + 1e-05)
    sum_x = (own[:, :256] + came[:, :256]) * norm
    sum_bc = (sum_bc + came[:, 256:512]) * norm
    sum_dt = (own[:, 384:388] + fine[:, :4]) * norm

    half = 128
    inputs_low = sum_x.astype(BF).reshape(2, half, 1, 4, 64)
    inputs = inputs_low.astype(F32)
    bc_round = sum_bc.astype(BF).reshape(2, half, 1, 256)
    b_low = bc_round[..., :128]
    c_low = bc_round[..., 128:]
    steps = jax.nn.softplus(sum_dt + dt_bias).reshape(2, half, 1, 4)
    rates = -jnp.exp(decay_log).reshape(1, 4)
    cumul = jnp.transpose(jnp.cumsum(steps * rates, axis=1), (0, 2, 3, 1))
    step_rows = jnp.transpose(steps, (0, 2, 3, 1))
    gram = jnp.einsum("ckgn,csgn->cgks", c_low, b_low, preferred_element_type=F32)
    places = jnp.arange(half, dtype=jnp.int32)
    causal = places[None, :] <= places[:, None]
    gaps = cumul[..., :, None] - cumul[..., None, :]
    decay = jnp.where(causal, jnp.exp(jnp.where(causal, gaps, 0.0)), 0.0)
    mixing = gram[:, :, None] * decay * step_rows[..., None, :]
    inner = split_product("cgjks,csgjp->ckgjp", mixing, inputs_low)
    last = cumul[..., -1]
    tail = jnp.exp(last[..., None] - cumul) * step_rows
    weighted = jnp.transpose(tail, (0, 3, 1, 2))[..., None] * inputs
    block_state = split_product("csgjp,csgn->cgjpn", weighted, b_low)
    block_decay = jnp.exp(last)

    rows = jnp.transpose(block_state.reshape(2, 32, 8, 128), (1, 0, 2, 3)).reshape(32, 16, 128)
    decays = jnp.repeat(block_decay.reshape(2, 4).T, 8, axis=0)
    decays = jnp.broadcast_to(decays[..., None], (32, 2, 128))
    sent = jnp.concatenate([rows, decays, jnp.zeros((32, 6, 128), F32)], axis=1)
    came = exchange(sent, CTX)
    entering = pl.pallas_call(
        scan,
        out_shape=jax.ShapeDtypeStruct((32, 16, 128), F32),
        in_specs=[VM],
        out_specs=VM,
        name="scan",
    )(came)
    entering = exchange(entering, CTX)
    entering = jnp.transpose(entering.reshape(32, 2, 8, 128), (1, 0, 2, 3)).reshape(2, 1, 4, 64, 128)

    carried = jnp.transpose(jnp.exp(cumul), (0, 3, 1, 2))[..., None] * split_product(
        "cgjpn,ckgn->ckgjp", entering, c_low
    )
    output = inner + carried + skip_gain.reshape(1, 4)[:, :, None] * inputs
    mamba_out = output.reshape(256, 256).astype(BF)
    return (residual_out, mamba_out)


def solution(mesh):
    fine = Mesh(mesh.devices.reshape(SIZES), AXES)
    placed = (
        P(CTX, TP),
        P(CTX, None, None),
        P(CTX, None, None),
        P(CTX, None),
        P(TP, None),
        P(),
        P(CTX, TP),
        P(CTX, None, None),
        P(CTX, TP),
        P(TP),
        P(TP),
        P(TP),
    )
    return jax.shard_map(
        body,
        mesh=fine,
        in_specs=placed,
        out_specs=(P(CTX, TP), P(CTX, TP)),
        check_vma=False,
    )
```

```python
import math

import jax
import jax.numpy as jnp
from jax import lax
from jax.experimental import pallas as pl
from jax.experimental.pallas import tpu as pltpu
from jax.sharding import Mesh
from jax.sharding import PartitionSpec as P

AXES = ("x", "zhh", "zhl", "co", "yhi", "ylo", "zl")
SIZES = (4, 2, 2, 2, 4, 2, 2)
ZH = ("zhh", "zhl")
CTX = ("x", "zhh", "zhl", "co")
Y = ("yhi", "ylo")
TP = ("yhi", "ylo", "zl")
BF = jnp.bfloat16
F32 = jnp.float32
LOWEST = -1e30


def split3(value):
    first = value.astype(BF)
    rest = value - first.astype(F32)
    second = rest.astype(BF)
    third = (rest - second.astype(F32)).astype(BF)
    return first, second, third


def features(value, zl):
    return jnp.concatenate(
        [
            lax.dynamic_slice_in_dim(value, 512 * i + 256 * zl, 256, 1)
            for i in range(8)
        ],
        axis=1,
    )


def swap(value, axis):
    return lax.ppermute(value, axis, [(0, 1), (1, 0)])


def exchange(value, axes):
    return lax.all_to_all(value, axes, split_axis=0, concat_axis=0, tiled=True)


def split_product(form, wide, narrow):
    upper = wide.astype(BF)
    lower = (wide - upper.astype(F32)).astype(BF)
    first_term = jnp.einsum(form, upper, narrow, preferred_element_type=F32)
    return first_term + jnp.einsum(form, lower, narrow, preferred_element_type=F32)


def pick(spots, q_ref, w_hbm, home_ref, away_ref, rest_ref, sems):
    zl, co = spots[2], spots[3]
    copies = []
    for at, (out_ref, side, half) in enumerate(
        ((home_ref, zl, co), (away_ref, 1 - zl, co), (rest_ref, zl, 1 - co))
    ):
        for i in range(4):
            start = pl.multiple_of(2048 * half + 512 * i + 256 * side, 256)
            copies.append(
                pltpu.make_async_copy(
                    w_hbm.at[:, pl.ds(start, 256)],
                    out_ref.at[:128, 256 * i : 256 * (i + 1)],
                    sems.at[4 * at + i],
                )
            )
    for copy in copies:
        copy.start()
    for i in range(8):
        block = q_ref[32 * i : 32 * (i + 1)]
        home_ref[128:, 128 * i : 128 * (i + 1)] = block
        away_ref[128:, 128 * i : 128 * (i + 1)] = block
    for copy in copies:
        copy.wait()


def attend(spots, home_ref, zl_ref, ylo_ref, both_ref, kv_ref, kv_co_ref, out_ref):
    ctx, quarter, co = spots[0], spots[1], spots[3]
    lane = lax.broadcasted_iota(jnp.int32, (32, 256), 1)
    token = lane % 128 // 32 * 64 + lane // 128 * 32 + lane % 32
    seat = jnp.where(token < 128, ctx, 63 - ctx) * 128 + token % 128
    reach = seat - lax.broadcasted_iota(jnp.int32, (32, 256), 0) - 32 * quarter

    def rows(chunk, start):
        ref = kv_ref if chunk < 4 else kv_co_ref
        first = chunk % 4 * 4
        return jnp.concatenate([ref[first + i, start : start + 64] for i in range(4)])

    levels = []
    for head in range(4):
        tiles = []
        query = jnp.concatenate(
            [
                (home_ref, zl_ref, ylo_ref, both_ref)[head][128:, 128 * i : 128 * (i + 1)]
                for i in (0, 2, 4, 6, 1, 3, 5, 7)
            ]
        )
        for chunk in range(8):
            scores = lax.dot_general(
                rows(chunk, 0),
                query,
                (((1,), (1,)), ((), ())),
                preferred_element_type=F32,
            ) * (math.log2(math.e) / math.sqrt(128))
            for piece in range(8):
                core = co if chunk < 4 else 1 - co
                source = (chunk % 4 * 4 + piece // 2) * 2 + core
                block = source if piece % 2 == 0 else 63 - source
                allowed = reach >= block * 128
                tiles.append(
                    jnp.where(allowed, scores[32 * piece : 32 * (piece + 1)], LOWEST)
                )
        top = tiles[0]
        for tile in tiles[1:]:
            top = jnp.maximum(top, tile)
        top = jnp.max(top, axis=0, keepdims=True)
        total = jnp.zeros((32, 256), F32)
        summed = jnp.zeros((128, 256), F32)
        for chunk in range(8):
            raised = [jnp.exp2(tile - top) for tile in tiles[8 * chunk : 8 * chunk + 8]]
            for part in raised:
                total = total + part
            summed = summed + lax.dot_general(
                rows(chunk, 64),
                jnp.concatenate(raised).astype(BF),
                (((0,), (0,)), ((), ())),
                preferred_element_type=F32,
            )
        total = jnp.sum(total, axis=0, keepdims=True)
        share = (summed / total).astype(BF)
        for dest in range(4):
            half = dest // 2
            out_ref[dest, 128 * head : 128 * (head + 1)] = share[:, 128 * half : 128 * half + 128]
        levels.append(jnp.where(top > 0.5 * LOWEST, top + jnp.log2(total), LOWEST))
    level = jnp.concatenate(levels)
    fine = jnp.concatenate([*split3(level), jnp.zeros((4, 256), BF)])
    for dest in range(4):
        half = dest // 2
        out_ref[dest, 512:528] = fine[:, 128 * half : 128 * half + 128]


def project(spots, came_ref, *refs):
    quarter, co = spots[1], spots[3]
    own_refs, rest_refs, out_ref, attended = refs[:4], refs[4:8], refs[8], refs[9]
    fine = [came_ref[source, 512:528].astype(F32) for source in range(4)]
    levels = [(part[8:12] + part[4:8]) + part[0:4] for part in fine]
    for head in range(4):
        level = [levels[s][head ^ s : (head ^ s) + 1] for s in range(4)]
        top = jnp.maximum(jnp.maximum(level[0], level[1]), jnp.maximum(level[2], level[3]))
        scales = [jnp.exp2(one - top) for one in level]
        total = (scales[0] + scales[1]) + (scales[2] + scales[3])
        joined = jnp.zeros((128, 128), F32)
        for source in range(4):
            slot = 128 * (head ^ source)
            joined = joined + (scales[source] / total) * came_ref[
                source, slot : slot + 128
            ].astype(F32)
        attended[head] = joined.astype(BF)
    four = jnp.concatenate([attended[quarter ^ r] for r in range(4)])

    def times(w_refs):
        rows = jnp.concatenate([w_ref[:128] for w_ref in w_refs])
        return lax.dot_general(
            four, rows, (((0,), (0,)), ((), ())), preferred_element_type=F32
        ).astype(BF)

    out_ref[:, pl.ds(pl.multiple_of(1024 * co, 1024), 1024)] = times(own_refs)
    out_ref[:, pl.ds(pl.multiple_of(1024 * (1 - co), 1024), 1024)] = times(rest_refs)


def scan(came_ref, out_ref):
    state = jnp.zeros((8, 128), F32)
    for i in range(32):
        out_ref[i, :8] = state
        state = came_ref[i, 16:17] * state + came_ref[i, :8]
    for i in range(31, -1, -1):
        out_ref[i, 8:] = state
        state = came_ref[i, 17:18] * state + came_ref[i, 8:16]


VM = pl.BlockSpec(memory_space=pltpu.VMEM)
SM = pl.BlockSpec(memory_space=pltpu.SMEM)
HB = pl.BlockSpec(memory_space=pl.ANY)


def body(
    queries,
    key_heads,
    head_values,
    hidden,
    out_proj,
    norm_gain,
    x_proj,
    bc_proj,
    dt_proj,
    dt_bias,
    decay_log,
    skip_gain,
):
    ctx = lax.axis_index(CTX)
    group = lax.axis_index("yhi")
    ylo = lax.axis_index("ylo")
    zl = lax.axis_index("zl")
    y = lax.axis_index(Y)
    quarter = 2 * ylo + zl

    bc_half = lax.dynamic_slice(bc_proj, (0, group, 128 * zl), (128, 1, 128))[:, 0]
    packed = jnp.concatenate(
        [x_proj, bc_half, jnp.pad(dt_proj, ((0, 0), (0, 124)))], axis=1
    )
    packed = lax.ppermute(packed, ("zhl", "zl"), [(0, 0), (1, 2), (2, 1), (3, 3)])
    spots = jnp.stack([ctx, quarter, zl, lax.axis_index("co")]).astype(jnp.int32)

    home, away, rest = pl.pallas_call(
        pick,
        out_shape=(
            jax.ShapeDtypeStruct((160, 1024), BF),
            jax.ShapeDtypeStruct((160, 1024), BF),
            jax.ShapeDtypeStruct((128, 1024), BF),
        ),
        in_specs=[SM, VM, HB],
        out_specs=(VM, VM, VM),
        scratch_shapes=[pltpu.SemaphoreType.DMA((12,))],
        name="pick",
    )(spots, queries, out_proj)

    def part(heads):
        return lax.dynamic_slice(
            heads.reshape(2, 128, 4, 128), (0, 32 * quarter, group, 0), (2, 32, 1, 128)
        ).reshape(64, 128)

    both = jnp.concatenate([part(key_heads), part(head_values)])
    both = jnp.broadcast_to(both, (16, 128, 128)).reshape(2048, 128)
    both = exchange(both, ("x", "zhh", "zhl")).reshape(16, 128, 128)
    near = [
        swap(away, "zl"),
        swap(home, "ylo"),
        lax.ppermute(away, ("ylo", "zl"), [(0, 3), (1, 2), (2, 1), (3, 0)]),
    ]
    both, near, packed = lax.optimization_barrier((both, near, packed))
    both_co = swap(both, "co")
    weights = lax.all_gather(packed, ("zhl", "x", "zhh", "co"), axis=0, tiled=True)
    weights = weights.reshape(2, 2048, 512)
    near_co = [swap(part, "co") for part in near]

    sent = pl.pallas_call(
        attend,
        out_shape=jax.ShapeDtypeStruct((4, 528, 128), BF),
        in_specs=[SM] + [VM] * 6,
        out_specs=VM,
        compiler_params=pltpu.CompilerParams(vmem_limit_bytes=32 << 20),
        name="attend",
    )(spots, home, *near, both, both_co)
    came = exchange(sent.reshape(4 * 528, 128), ("ylo", "zl")).reshape(4, 528, 128)
    head_part = pl.pallas_call(
        project,
        out_shape=jax.ShapeDtypeStruct((128, 2048), BF),
        in_specs=[SM] + [VM] * 9,
        out_specs=VM,
        scratch_shapes=[pltpu.VMEM((4, 128, 128), BF)],
        compiler_params=pltpu.CompilerParams(vmem_limit_bytes=32 << 20),
        name="project",
    )(spots, came, home, *near, rest, *near_co)

    parts = exchange(head_part, "yhi").reshape(4, 32, 2048)
    attention_sum = jnp.sum(parts.astype(F32), axis=0)
    hidden_mine = features(lax.dynamic_slice(hidden, (32 * y, 0), (32, 4096)), zl)
    residual = (hidden_mine.astype(F32) + attention_sum).astype(BF)
    spread = jnp.broadcast_to(residual[None], (8, 32, 2048)).reshape(256, 2048)
    residual = exchange(spread, Y)
    residual_out = lax.dynamic_slice(residual, (0, 256 * y), (256, 256))

    gain = lax.dynamic_index_in_dim(norm_gain.reshape(8, 2, 256), zl, 1, keepdims=False)
    as_float = residual.astype(F32)
    square = jnp.sum(as_float * as_float, axis=-1, keepdims=True)
    gained = (as_float * gain.reshape(1, 2048)).astype(BF)
    sums = jnp.einsum("tk,zkn->ztn", gained, weights, preferred_element_type=F32)
    own = lax.dynamic_index_in_dim(sums, zl, 0, keepdims=False)
    away = lax.dynamic_index_in_dim(sums, 1 - zl, 0, keepdims=False)
    sum_bc = jnp.concatenate([sums[0, :, 256:384], sums[1, :, 256:384]], axis=1)
    fine = jnp.concatenate(split3(jnp.concatenate([away[:, 384:388], square], axis=1)), axis=1)
    sent = jnp.concatenate(
        [away[:, :256].astype(BF), sum_bc.astype(BF), jnp.pad(fine, ((0, 0), (0, 113)))], axis=1
    )
    came = swap(sent, "zl").astype(F32)
    fine = came[:, 512:527].reshape(256, 3, 5)
    fine = (fine[:, 2] + fine[:, 1]) + fine[:, 0]
    norm = lax.rsqrt((square + fine[:, 4:5]) / 4096.0 + 1e-05)
    sum_x = (own[:, :256] + came[:, :256]) * norm
    sum_bc = (sum_bc + came[:, 256:512]) * norm
    sum_dt = (own[:, 384:388] + fine[:, :4]) * norm

    half = 128
    inputs_low = sum_x.astype(BF).reshape(2, half, 1, 4, 64)
    inputs = inputs_low.astype(F32)
    bc_round = sum_bc.astype(BF).reshape(2, half, 1, 256)
    b_low = bc_round[..., :128]
    c_low = bc_round[..., 128:]
    steps = jax.nn.softplus(sum_dt + dt_bias).reshape(2, half, 1, 4)
    rates = -jnp.exp(decay_log).reshape(1, 4)
    cumul = jnp.transpose(jnp.cumsum(steps * rates, axis=1), (0, 2, 3, 1))
    step_rows = jnp.transpose(steps, (0, 2, 3, 1))
    gram = jnp.einsum("ckgn,csgn->cgks", c_low, b_low, preferred_element_type=F32)
    places = jnp.arange(half, dtype=jnp.int32)
    causal = places[None, :] <= places[:, None]
    gaps = cumul[..., :, None] - cumul[..., None, :]
    decay = jnp.where(causal, jnp.exp(jnp.where(causal, gaps, 0.0)), 0.0)
    mixing = gram[:, :, None] * decay * step_rows[..., None, :]
    inner = split_product("cgjks,csgjp->ckgjp", mixing, inputs_low)
    last = cumul[..., -1]
    tail = jnp.exp(last[..., None] - cumul) * step_rows
    weighted = jnp.transpose(tail, (0, 3, 1, 2))[..., None] * inputs
    block_state = split_product("csgjp,csgn->cgjpn", weighted, b_low)
    block_decay = jnp.exp(last)

    rows = jnp.transpose(block_state.reshape(2, 32, 8, 128), (1, 0, 2, 3)).reshape(32, 16, 128)
    decays = jnp.repeat(block_decay.reshape(2, 4).T, 8, axis=0)
    decays = jnp.broadcast_to(decays[..., None], (32, 2, 128))
    sent = jnp.concatenate([rows, decays, jnp.zeros((32, 6, 128), F32)], axis=1)
    came = exchange(sent, CTX)
    entering = pl.pallas_call(
        scan,
        out_shape=jax.ShapeDtypeStruct((32, 16, 128), F32),
        in_specs=[VM],
        out_specs=VM,
        name="scan",
    )(came)
    entering = exchange(entering, CTX)
    entering = jnp.transpose(entering.reshape(32, 2, 8, 128), (1, 0, 2, 3)).reshape(2, 1, 4, 64, 128)

    carried = jnp.transpose(jnp.exp(cumul), (0, 3, 1, 2))[..., None] * split_product(
        "cgjpn,ckgn->ckgjp", entering, c_low
    )
    output = inner + carried + skip_gain.reshape(1, 4)[:, :, None] * inputs
    mamba_out = output.reshape(256, 256).astype(BF)
    return (residual_out, mamba_out)


def solution(mesh):
    fine = Mesh(mesh.devices.reshape(SIZES), AXES)
    placed = (
        P(CTX, TP),
        P(CTX, None, None),
        P(CTX, None, None),
        P(CTX, None),
        P(TP, None),
        P(),
        P(CTX, TP),
        P(CTX, None, None),
        P(CTX, TP),
        P(TP),
        P(TP),
        P(TP),
    )
    return jax.shard_map(
        body,
        mesh=fine,
        in_specs=placed,
        out_specs=(P(CTX, TP), P(CTX, TP)),
        check_vma=False,
    )
```

```python
import math

import jax
import jax.numpy as jnp
from jax import lax
from jax.experimental import pallas as pl
from jax.experimental.pallas import tpu as pltpu
from jax.sharding import Mesh
from jax.sharding import PartitionSpec as P

AXES = ("x", "zhh", "zhl", "co", "yhi", "ylo", "zl")
SIZES = (4, 2, 2, 2, 4, 2, 2)
ZH = ("zhh", "zhl")
CTX = ("x", "zhh", "zhl", "co")
Y = ("yhi", "ylo")
TP = ("yhi", "ylo", "zl")
BF = jnp.bfloat16
F32 = jnp.float32
LOWEST = -1e30


def split3(value):
    first = value.astype(BF)
    rest = value - first.astype(F32)
    second = rest.astype(BF)
    third = (rest - second.astype(F32)).astype(BF)
    return first, second, third


def features(value, zl):
    return jnp.concatenate(
        [
            lax.dynamic_slice_in_dim(value, 512 * i + 256 * zl, 256, 1)
            for i in range(8)
        ],
        axis=1,
    )


def swap(value, axis):
    return lax.ppermute(value, axis, [(0, 1), (1, 0)])


def exchange(value, axes):
    return lax.all_to_all(value, axes, split_axis=0, concat_axis=0, tiled=True)


def split_product(form, wide, narrow):
    upper = wide.astype(BF)
    lower = (wide - upper.astype(F32)).astype(BF)
    first_term = jnp.einsum(form, upper, narrow, preferred_element_type=F32)
    return first_term + jnp.einsum(form, lower, narrow, preferred_element_type=F32)


def pick(spots, q_ref, w_hbm, home_ref, away_ref, rest_ref, sems):
    zl, co = spots[2], spots[3]
    copies = []
    for at, (out_ref, side, half) in enumerate(
        ((home_ref, zl, co), (away_ref, 1 - zl, co), (rest_ref, zl, 1 - co))
    ):
        for i in range(4):
            start = pl.multiple_of(2048 * half + 512 * i + 256 * side, 256)
            copies.append(
                pltpu.make_async_copy(
                    w_hbm.at[:, pl.ds(start, 256)],
                    out_ref.at[:128, 256 * i : 256 * (i + 1)],
                    sems.at[4 * at + i],
                )
            )
    for copy in copies:
        copy.start()
    for i in range(8):
        block = q_ref[32 * i : 32 * (i + 1)]
        home_ref[128:, 128 * i : 128 * (i + 1)] = block
        away_ref[128:, 128 * i : 128 * (i + 1)] = block
    for copy in copies:
        copy.wait()


def attend(spots, home_ref, zl_ref, ylo_ref, both_ref, kv_ref, kv_co_ref, out_ref):
    ctx, quarter, co = spots[0], spots[1], spots[3]
    lane = lax.broadcasted_iota(jnp.int32, (32, 128), 1)
    token = lane % 64 // 32 * 64 + lane // 64 * 32 + lane % 32
    reach = token - lax.broadcasted_iota(jnp.int32, (32, 128), 0) - 32 * quarter
    first_reach = reach + 128 * ctx
    second_reach = reach + 128 * (63 - ctx)

    def rows(chunk, start):
        ref = kv_ref if chunk < 2 else kv_co_ref
        first = chunk % 2 * 8
        return jnp.concatenate([ref[first + i, start : start + 32] for i in range(8)])

    def source(chunk, piece):
        return (chunk % 2 * 8 + piece) * 2 + (co if chunk < 2 else 1 - co)

    def peak(tiles):
        top = tiles[0]
        for tile in tiles[1:]:
            top = jnp.maximum(top, tile)
        return jnp.max(top, axis=0, keepdims=True)

    levels = []
    for head in range(4):
        q_ref = (home_ref, zl_ref, ylo_ref, both_ref)[head]
        query = jnp.concatenate(
            [
                q_ref[128:, 128 * i : 128 * (i + 1)]
                for i in (0, 2, 1, 3, 4, 6, 5, 7)
            ]
        )
        early, full, late = [], [], []
        for chunk in range(4):
            scores, later = [
                lax.dot_general(
                    rows(chunk, start),
                    some,
                    (((1,), (1,)), ((), ())),
                    preferred_element_type=F32,
                )
                * (math.log2(math.e) / math.sqrt(128))
                for start, some in ((0, query), (32, query[128:]))
            ]
            for piece in range(8):
                at = slice(32 * piece, 32 * (piece + 1))
                block = source(chunk, piece)
                early.append(
                    jnp.where(first_reach >= block * 128, scores[at, :128], LOWEST)
                )
                full.append(scores[at, 128:])
                late.append(
                    jnp.where(second_reach >= (63 - block) * 128, later[at], LOWEST)
                )
        tops = [peak(early), jnp.maximum(peak(full), peak(late))]
        totals = [jnp.zeros((32, 128), F32), jnp.zeros((32, 128), F32)]
        summed = jnp.zeros((128, 256), F32)
        added = jnp.zeros((128, 128), F32)
        for chunk in range(4):
            raised = [[], [], []]
            for piece in range(8 * chunk, 8 * chunk + 8):
                for i, (tiles, half) in enumerate(((early, 0), (full, 1), (late, 1))):
                    part = jnp.exp2(tiles[piece] - tops[half])
                    totals[half] = totals[half] + part
                    raised[i].append(part)
            raised = [jnp.concatenate(parts).astype(BF) for parts in raised]
            summed = summed + lax.dot_general(
                rows(chunk, 64),
                jnp.concatenate(raised[:2], axis=1),
                (((0,), (0,)), ((), ())),
                preferred_element_type=F32,
            )
            added = added + lax.dot_general(
                rows(chunk, 96), raised[2], (((0,), (0,)), ((), ())), preferred_element_type=F32
            )
        totals = [jnp.sum(total, axis=0, keepdims=True) for total in totals]
        share = [
            (summed[:, :128] / totals[0]).astype(BF),
            ((summed[:, 128:] + added) / totals[1]).astype(BF),
        ]
        for dest in range(4):
            at = slice(64 * (dest // 2), 64 * (dest // 2) + 64)
            out_ref[dest, 128 * head : 128 * (head + 1)] = jnp.concatenate(
                [part[:, at] for part in share], axis=1
            )
        levels.append(
            [
                jnp.where(top > 0.5 * LOWEST, top + jnp.log2(total), LOWEST)
                for top, total in zip(tops, totals)
            ]
        )
    for dest in range(4):
        at = slice(64 * (dest // 2), 64 * (dest // 2) + 64)
        level = jnp.concatenate(
            [jnp.concatenate([part[:, at] for part in pair], axis=1) for pair in levels]
        )
        out_ref[dest, 512:528] = jnp.concatenate([*split3(level), jnp.zeros((4, 128), BF)])


def project(spots, came_ref, *refs):
    quarter, co = spots[1], spots[3]
    own_refs, rest_refs, out_ref, attended = refs[:4], refs[4:8], refs[8], refs[9]
    fine = [came_ref[source, 512:528].astype(F32) for source in range(4)]
    levels = [(part[8:12] + part[4:8]) + part[0:4] for part in fine]
    for head in range(4):
        level = [levels[s][head ^ s : (head ^ s) + 1] for s in range(4)]
        top = jnp.maximum(jnp.maximum(level[0], level[1]), jnp.maximum(level[2], level[3]))
        scales = [jnp.exp2(one - top) for one in level]
        total = (scales[0] + scales[1]) + (scales[2] + scales[3])
        joined = jnp.zeros((128, 128), F32)
        for source in range(4):
            slot = 128 * (head ^ source)
            joined = joined + (scales[source] / total) * came_ref[
                source, slot : slot + 128
            ].astype(F32)
        attended[head] = joined.astype(BF)
    four = jnp.concatenate([attended[quarter ^ r] for r in range(4)])

    def times(w_refs):
        rows = jnp.concatenate([w_ref[:128] for w_ref in w_refs])
        return lax.dot_general(
            four, rows, (((0,), (0,)), ((), ())), preferred_element_type=F32
        ).astype(BF)

    out_ref[:, pl.ds(pl.multiple_of(1024 * co, 1024), 1024)] = times(own_refs)
    out_ref[:, pl.ds(pl.multiple_of(1024 * (1 - co), 1024), 1024)] = times(rest_refs)


def mix(spots, r_ref, gain_ref, w_ref, keep_ref, sent_ref):
    zl = spots[2]
    value = r_ref[...].astype(F32)
    square = jnp.sum(value * value, axis=1, keepdims=True)
    gained = (value * gain_ref[...]).astype(BF)

    def times(side):
        total = None
        for p in range(8):
            product = jnp.dot(
                gained[:, 256 * p : 256 * (p + 1)],
                w_ref[p, side],
                preferred_element_type=F32,
            )
            total = product if total is None else total + product
        return total

    sums = [times(0), times(1)]
    lane = lax.broadcasted_iota(jnp.int32, (256, 128), 1)
    for mine in range(2):
        one = jnp.where(zl == mine, sums[0], sums[1])
        bc = jnp.concatenate([sums[0][:, 256:384], sums[1][:, 256:384]], axis=1)
        fine = jnp.where(lane == 4, square, one[:, 384:])
        if mine == 0:
            keep_ref[:, :256] = one[:, :256]
            keep_ref[:, 256:512] = bc
            keep_ref[:, 512:] = fine
        else:
            first, second, third = [part.astype(F32) for part in split3(fine)]
            fine = first + pltpu.roll(second, 8, 1) + pltpu.roll(third, 16, 1)
            sent_ref[:, :256] = one[:, :256].astype(BF)
            sent_ref[:, 256:512] = bc.astype(BF)
            sent_ref[:, 512:] = fine.astype(BF)


def scan(came_ref, out_ref):
    state = jnp.zeros((8, 128), F32)
    for i in range(32):
        out_ref[i, :8] = state
        state = came_ref[i, 16:17] * state + came_ref[i, :8]
    for i in range(31, -1, -1):
        out_ref[i, 8:] = state
        state = came_ref[i, 17:18] * state + came_ref[i, 8:16]


VM = pl.BlockSpec(memory_space=pltpu.VMEM)
SM = pl.BlockSpec(memory_space=pltpu.SMEM)
HB = pl.BlockSpec(memory_space=pl.ANY)


def body(
    queries,
    key_heads,
    head_values,
    hidden,
    out_proj,
    norm_gain,
    x_proj,
    bc_proj,
    dt_proj,
    dt_bias,
    decay_log,
    skip_gain,
):
    ctx = lax.axis_index(CTX)
    group = lax.axis_index("yhi")
    ylo = lax.axis_index("ylo")
    zl = lax.axis_index("zl")
    y = lax.axis_index(Y)
    quarter = 2 * ylo + zl

    bc_half = lax.dynamic_slice(bc_proj, (0, group, 128 * zl), (128, 1, 128))[:, 0]
    packed = jnp.concatenate(
        [x_proj, bc_half, jnp.pad(dt_proj, ((0, 0), (0, 124)))], axis=1
    )
    packed = lax.ppermute(packed, ("zhl", "zl"), [(0, 0), (1, 2), (2, 1), (3, 3)])
    spots = jnp.stack([ctx, quarter, zl, lax.axis_index("co")]).astype(jnp.int32)

    home, away, rest = pl.pallas_call(
        pick,
        out_shape=(
            jax.ShapeDtypeStruct((160, 1024), BF),
            jax.ShapeDtypeStruct((160, 1024), BF),
            jax.ShapeDtypeStruct((128, 1024), BF),
        ),
        in_specs=[SM, VM, HB],
        out_specs=(VM, VM, VM),
        scratch_shapes=[pltpu.SemaphoreType.DMA((12,))],
        name="pick",
    )(spots, queries, out_proj)

    def part(heads):
        return lax.dynamic_slice(
            heads.reshape(2, 128, 4, 128), (0, 32 * quarter, group, 0), (2, 32, 1, 128)
        ).reshape(64, 128)

    both = jnp.concatenate([part(key_heads), part(head_values)])
    both = jnp.broadcast_to(both, (16, 128, 128)).reshape(2048, 128)
    both = exchange(both, ("x", "zhh", "zhl")).reshape(16, 128, 128)
    near = [
        swap(away, "zl"),
        swap(home, "ylo"),
        lax.ppermute(away, ("ylo", "zl"), [(0, 3), (1, 2), (2, 1), (3, 0)]),
    ]
    both, near, packed = lax.optimization_barrier((both, near, packed))
    both_co = swap(both, "co")
    weights = lax.all_gather(packed, CTX, axis=0, tiled=True).reshape(8, 2, 256, 512)
    near_co = [swap(part, "co") for part in near]

    sent = pl.pallas_call(
        attend,
        out_shape=jax.ShapeDtypeStruct((4, 528, 128), BF),
        in_specs=[SM] + [VM] * 6,
        out_specs=VM,
        compiler_params=pltpu.CompilerParams(vmem_limit_bytes=32 << 20),
        name="attend",
    )(spots, home, *near, both, both_co)
    came = exchange(sent.reshape(4 * 528, 128), ("ylo", "zl")).reshape(4, 528, 128)
    head_part = pl.pallas_call(
        project,
        out_shape=jax.ShapeDtypeStruct((128, 2048), BF),
        in_specs=[SM] + [VM] * 9,
        out_specs=VM,
        scratch_shapes=[pltpu.VMEM((4, 128, 128), BF)],
        compiler_params=pltpu.CompilerParams(vmem_limit_bytes=32 << 20),
        name="project",
    )(spots, came, home, *near, rest, *near_co)

    parts = exchange(head_part, "yhi").reshape(4, 32, 2048)
    attention_sum = jnp.sum(parts.astype(F32), axis=0)
    hidden_mine = features(lax.dynamic_slice(hidden, (32 * y, 0), (32, 4096)), zl)
    residual = (hidden_mine.astype(F32) + attention_sum).astype(BF)
    spread = jnp.broadcast_to(residual[None], (8, 32, 2048)).reshape(256, 2048)
    residual = exchange(spread, Y)
    residual_out = lax.dynamic_slice(residual, (0, 256 * y), (256, 256))

    gain = features(norm_gain[None], zl)
    keep, sent = pl.pallas_call(
        mix,
        out_shape=(
            jax.ShapeDtypeStruct((256, 640), F32),
            jax.ShapeDtypeStruct((256, 640), BF),
        ),
        in_specs=[SM] + [VM] * 3,
        out_specs=(VM, VM),
        compiler_params=pltpu.CompilerParams(vmem_limit_bytes=32 << 20),
        name="mix",
    )(spots, residual, gain, weights)
    came = swap(sent, "zl").astype(F32)
    fine = (came[:, 528:533] + came[:, 520:525]) + came[:, 512:517]
    fine = keep[:, 512:517] + fine
    norm = lax.rsqrt(fine[:, 4:5] / 4096.0 + 1e-05)
    sum_x = (keep[:, :256] + came[:, :256]) * norm
    sum_bc = (keep[:, 256:512] + came[:, 256:512]) * norm
    sum_dt = fine[:, :4] * norm

    half = 128
    inputs_low = sum_x.astype(BF).reshape(2, half, 1, 4, 64)
    inputs = inputs_low.astype(F32)
    bc_round = sum_bc.astype(BF).reshape(2, half, 1, 256)
    b_low = bc_round[..., :128]
    c_low = bc_round[..., 128:]
    steps = jax.nn.softplus(sum_dt + dt_bias).reshape(2, half, 1, 4)
    rates = -jnp.exp(decay_log).reshape(1, 4)
    cumul = jnp.transpose(jnp.cumsum(steps * rates, axis=1), (0, 2, 3, 1))
    step_rows = jnp.transpose(steps, (0, 2, 3, 1))
    gram = jnp.einsum("ckgn,csgn->cgks", c_low, b_low, preferred_element_type=F32)
    places = jnp.arange(half, dtype=jnp.int32)
    causal = places[None, :] <= places[:, None]
    gaps = cumul[..., :, None] - cumul[..., None, :]
    decay = jnp.where(causal, jnp.exp(jnp.where(causal, gaps, 0.0)), 0.0)
    mixing = gram[:, :, None] * decay * step_rows[..., None, :]
    inner = split_product("cgjks,csgjp->ckgjp", mixing, inputs_low)
    last = cumul[..., -1]
    tail = jnp.exp(last[..., None] - cumul) * step_rows
    weighted = jnp.transpose(tail, (0, 3, 1, 2))[..., None] * inputs
    block_state = split_product("csgjp,csgn->cgjpn", weighted, b_low)
    block_decay = jnp.exp(last)

    rows = jnp.transpose(block_state.reshape(2, 32, 8, 128), (1, 0, 2, 3)).reshape(32, 16, 128)
    decays = jnp.repeat(block_decay.reshape(2, 4).T, 8, axis=0)
    decays = jnp.broadcast_to(decays[..., None], (32, 2, 128))
    sent = jnp.concatenate([rows, decays, jnp.zeros((32, 6, 128), F32)], axis=1)
    came = exchange(sent, CTX)
    entering = pl.pallas_call(
        scan,
        out_shape=jax.ShapeDtypeStruct((32, 16, 128), F32),
        in_specs=[VM],
        out_specs=VM,
        name="scan",
    )(came)
    entering = exchange(entering, CTX)
    entering = jnp.transpose(entering.reshape(32, 2, 8, 128), (1, 0, 2, 3)).reshape(2, 1, 4, 64, 128)

    carried = jnp.transpose(jnp.exp(cumul), (0, 3, 1, 2))[..., None] * split_product(
        "cgjpn,ckgn->ckgjp", entering, c_low
    )
    output = inner + carried + skip_gain.reshape(1, 4)[:, :, None] * inputs
    mamba_out = output.reshape(256, 256).astype(BF)
    return (residual_out, mamba_out)


def solution(mesh):
    fine = Mesh(mesh.devices.reshape(SIZES), AXES)
    placed = (
        P(CTX, TP),
        P(CTX, None, None),
        P(CTX, None, None),
        P(CTX, None),
        P(TP, None),
        P(),
        P(CTX, TP),
        P(CTX, None, None),
        P(CTX, TP),
        P(TP),
        P(TP),
        P(TP),
    )
    return jax.shard_map(
        body,
        mesh=fine,
        in_specs=placed,
        out_specs=(P(CTX, TP), P(CTX, TP)),
        check_vma=False,
    )
```

```python
import math

import jax
import jax.numpy as jnp
from jax import lax
from jax.experimental import pallas as pl
from jax.experimental.pallas import tpu as pltpu
from jax.sharding import Mesh
from jax.sharding import PartitionSpec as P

AXES = ("x", "zhh", "zhl", "co", "yhi", "ylo", "zl")
SIZES = (4, 2, 2, 2, 4, 2, 2)
ZH = ("zhh", "zhl")
CTX = ("x", "zhh", "zhl", "co")
Y = ("yhi", "ylo")
TP = ("yhi", "ylo", "zl")
BF = jnp.bfloat16
F32 = jnp.float32
LOWEST = -1e30


def split3(value):
    first = value.astype(BF)
    rest = value - first.astype(F32)
    second = rest.astype(BF)
    third = (rest - second.astype(F32)).astype(BF)
    return first, second, third


def features(value, zl):
    return jnp.concatenate(
        [
            lax.dynamic_slice_in_dim(value, 512 * i + 256 * zl, 256, 1)
            for i in range(8)
        ],
        axis=1,
    )


def swap(value, axis):
    return lax.ppermute(value, axis, [(0, 1), (1, 0)])


def exchange(value, axes):
    return lax.all_to_all(value, axes, split_axis=0, concat_axis=0, tiled=True)


def split_product(form, wide, narrow):
    upper = wide.astype(BF)
    lower = (wide - upper.astype(F32)).astype(BF)
    first_term = jnp.einsum(form, upper, narrow, preferred_element_type=F32)
    return first_term + jnp.einsum(form, lower, narrow, preferred_element_type=F32)


def pick(spots, q_ref, w_hbm, home_ref, away_ref, rest_ref, sems):
    zl, co = spots[2], spots[3]
    copies = []
    for at, (out_ref, side, half) in enumerate(
        ((home_ref, zl, co), (away_ref, 1 - zl, co), (rest_ref, zl, 1 - co))
    ):
        for i in range(4):
            start = pl.multiple_of(2048 * half + 512 * i + 256 * side, 256)
            copies.append(
                pltpu.make_async_copy(
                    w_hbm.at[:, pl.ds(start, 256)],
                    out_ref.at[:128, 256 * i : 256 * (i + 1)],
                    sems.at[4 * at + i],
                )
            )
    for copy in copies:
        copy.start()
    for i in range(8):
        block = q_ref[32 * i : 32 * (i + 1)]
        home_ref[128:, 128 * i : 128 * (i + 1)] = block
        away_ref[128:, 128 * i : 128 * (i + 1)] = block
    for copy in copies:
        copy.wait()


def attend(spots, home_ref, zl_ref, ylo_ref, both_ref, kv_ref, kv_co_ref, out_ref):
    ctx, quarter, co = spots[0], spots[1], spots[3]
    lane = lax.broadcasted_iota(jnp.int32, (32, 128), 1)
    token = lane % 64 // 32 * 64 + lane // 64 * 32 + lane % 32
    reach = token - lax.broadcasted_iota(jnp.int32, (32, 128), 0) - 32 * quarter
    first_reach = reach + 128 * ctx
    second_reach = reach + 128 * (63 - ctx)

    def rows(chunk, start):
        ref = kv_ref if chunk < 2 else kv_co_ref
        first = chunk % 2 * 8
        return jnp.concatenate([ref[first + i, start : start + 32] for i in range(8)])

    def source(chunk, piece):
        return (chunk % 2 * 8 + piece) * 2 + (co if chunk < 2 else 1 - co)

    def peak(tiles):
        top = tiles[0]
        for tile in tiles[1:]:
            top = jnp.maximum(top, tile)
        return jnp.max(top, axis=0, keepdims=True)

    levels = []
    for head in range(4):
        q_ref = (home_ref, zl_ref, ylo_ref, both_ref)[head]
        query = jnp.concatenate(
            [
                q_ref[128:, 128 * i : 128 * (i + 1)]
                for i in (0, 2, 1, 3, 4, 6, 5, 7)
            ]
        )
        early, full, late = [], [], []
        for chunk in range(4):
            scores, later = [
                lax.dot_general(
                    rows(chunk, start),
                    some,
                    (((1,), (1,)), ((), ())),
                    preferred_element_type=F32,
                )
                * (math.log2(math.e) / math.sqrt(128))
                for start, some in ((0, query), (32, query[128:]))
            ]
            for piece in range(8):
                at = slice(32 * piece, 32 * (piece + 1))
                block = source(chunk, piece)
                early.append(
                    jnp.where(first_reach >= block * 128, scores[at, :128], LOWEST)
                )
                full.append(scores[at, 128:])
                late.append(
                    jnp.where(second_reach >= (63 - block) * 128, later[at], LOWEST)
                )
        tops = [peak(early), jnp.maximum(peak(full), peak(late))]
        totals = [jnp.zeros((32, 128), F32), jnp.zeros((32, 128), F32)]
        summed = jnp.zeros((128, 256), F32)
        added = jnp.zeros((128, 128), F32)
        for chunk in range(4):
            raised = [[], [], []]
            for piece in range(8 * chunk, 8 * chunk + 8):
                for i, (tiles, half) in enumerate(((early, 0), (full, 1), (late, 1))):
                    part = jnp.exp2(tiles[piece] - tops[half])
                    totals[half] = totals[half] + part
                    raised[i].append(part)
            raised = [jnp.concatenate(parts).astype(BF) for parts in raised]
            summed = summed + lax.dot_general(
                rows(chunk, 64),
                jnp.concatenate(raised[:2], axis=1),
                (((0,), (0,)), ((), ())),
                preferred_element_type=F32,
            )
            added = added + lax.dot_general(
                rows(chunk, 96), raised[2], (((0,), (0,)), ((), ())), preferred_element_type=F32
            )
        totals = [jnp.sum(total, axis=0, keepdims=True) for total in totals]
        share = [
            (summed[:, :128] / totals[0]).astype(BF),
            ((summed[:, 128:] + added) / totals[1]).astype(BF),
        ]
        for dest in range(4):
            at = slice(64 * (dest // 2), 64 * (dest // 2) + 64)
            out_ref[dest, 128 * head : 128 * (head + 1)] = jnp.concatenate(
                [part[:, at] for part in share], axis=1
            )
        levels.append(
            [
                jnp.where(top > 0.5 * LOWEST, top + jnp.log2(total), LOWEST)
                for top, total in zip(tops, totals)
            ]
        )
    for dest in range(4):
        at = slice(64 * (dest // 2), 64 * (dest // 2) + 64)
        level = jnp.concatenate(
            [jnp.concatenate([part[:, at] for part in pair], axis=1) for pair in levels]
        )
        out_ref[dest, 512:528] = jnp.concatenate([*split3(level), jnp.zeros((4, 128), BF)])


def project(spots, came_ref, *refs):
    quarter, co = spots[1], spots[3]
    own_refs, rest_refs, out_ref, attended = refs[:4], refs[4:8], refs[8], refs[9]
    fine = [came_ref[source, 512:528].astype(F32) for source in range(4)]
    levels = [(part[8:12] + part[4:8]) + part[0:4] for part in fine]
    for head in range(4):
        level = [levels[s][head ^ s : (head ^ s) + 1] for s in range(4)]
        top = jnp.maximum(jnp.maximum(level[0], level[1]), jnp.maximum(level[2], level[3]))
        scales = [jnp.exp2(one - top) for one in level]
        total = (scales[0] + scales[1]) + (scales[2] + scales[3])
        joined = jnp.zeros((128, 128), F32)
        for source in range(4):
            slot = 128 * (head ^ source)
            joined = joined + (scales[source] / total) * came_ref[
                source, slot : slot + 128
            ].astype(F32)
        attended[head] = joined.astype(BF)
    four = jnp.concatenate([attended[quarter ^ r] for r in range(4)])

    def times(w_refs):
        rows = jnp.concatenate([w_ref[:128] for w_ref in w_refs])
        return lax.dot_general(
            four, rows, (((0,), (0,)), ((), ())), preferred_element_type=F32
        ).astype(BF)

    out_ref[:, pl.ds(pl.multiple_of(1024 * co, 1024), 1024)] = times(own_refs)
    out_ref[:, pl.ds(pl.multiple_of(1024 * (1 - co), 1024), 1024)] = times(rest_refs)


def mix(spots, r_ref, gain_ref, w_ref, keep_ref, sent_ref):
    zl = spots[2]
    value = r_ref[...].astype(F32)
    square = jnp.sum(value * value, axis=1, keepdims=True)
    gained = (value * gain_ref[...]).astype(BF)

    def times(side):
        total = None
        for p in range(8):
            product = jnp.dot(
                gained[:, 256 * p : 256 * (p + 1)],
                w_ref[p, side],
                preferred_element_type=F32,
            )
            total = product if total is None else total + product
        return total

    sums = [times(0), times(1)]
    lane = lax.broadcasted_iota(jnp.int32, (256, 128), 1)
    for mine in range(2):
        one = jnp.where(zl == mine, sums[0], sums[1])
        bc = jnp.concatenate([sums[0][:, 256:384], sums[1][:, 256:384]], axis=1)
        fine = jnp.where(lane == 4, square, one[:, 384:])
        if mine == 0:
            keep_ref[:, :256] = one[:, :256]
            keep_ref[:, 256:512] = bc
            keep_ref[:, 512:] = fine
        else:
            first, second, third = [part.astype(F32) for part in split3(fine)]
            fine = first + pltpu.roll(second, 8, 1) + pltpu.roll(third, 16, 1)
            sent_ref[:, :256] = one[:, :256].astype(BF)
            sent_ref[:, 256:512] = bc.astype(BF)
            sent_ref[:, 512:] = fine.astype(BF)


def scan(came_ref, out_ref):
    state = jnp.zeros((8, 128), F32)
    fine = [came_ref[i, 16:32].astype(F32) for i in range(32)]
    rows = [came_ref[i, :16].astype(F32) for i in range(32)]
    entering = []
    for i in range(32):
        entering.append(state)
        decay = (fine[i][4:5] + fine[i][2:3]) + fine[i][0:1]
        state = decay * state + rows[i][:8]
    for i in range(31, -1, -1):
        out_ref[i] = jnp.concatenate([entering[i], state]).astype(BF)
        decay = (fine[i][5:6] + fine[i][3:4]) + fine[i][1:2]
        state = decay * state + rows[i][8:]


VM = pl.BlockSpec(memory_space=pltpu.VMEM)
SM = pl.BlockSpec(memory_space=pltpu.SMEM)
HB = pl.BlockSpec(memory_space=pl.ANY)


def body(
    queries,
    key_heads,
    head_values,
    hidden,
    out_proj,
    norm_gain,
    x_proj,
    bc_proj,
    dt_proj,
    dt_bias,
    decay_log,
    skip_gain,
):
    ctx = lax.axis_index(CTX)
    group = lax.axis_index("yhi")
    ylo = lax.axis_index("ylo")
    zl = lax.axis_index("zl")
    y = lax.axis_index(Y)
    quarter = 2 * ylo + zl

    bc_half = lax.dynamic_slice(bc_proj, (0, group, 128 * zl), (128, 1, 128))[:, 0]
    packed = jnp.concatenate(
        [x_proj, bc_half, jnp.pad(dt_proj, ((0, 0), (0, 124)))], axis=1
    )
    packed = lax.ppermute(packed, ("zhl", "zl"), [(0, 0), (1, 2), (2, 1), (3, 3)])
    spots = jnp.stack([ctx, quarter, zl, lax.axis_index("co")]).astype(jnp.int32)

    home, away, rest = pl.pallas_call(
        pick,
        out_shape=(
            jax.ShapeDtypeStruct((160, 1024), BF),
            jax.ShapeDtypeStruct((160, 1024), BF),
            jax.ShapeDtypeStruct((128, 1024), BF),
        ),
        in_specs=[SM, VM, HB],
        out_specs=(VM, VM, VM),
        scratch_shapes=[pltpu.SemaphoreType.DMA((12,))],
        name="pick",
    )(spots, queries, out_proj)

    def part(heads):
        return lax.dynamic_slice(
            heads.reshape(2, 128, 4, 128), (0, 32 * quarter, group, 0), (2, 32, 1, 128)
        ).reshape(64, 128)

    both = jnp.concatenate([part(key_heads), part(head_values)])
    both = jnp.broadcast_to(both, (16, 128, 128)).reshape(2048, 128)
    both = exchange(both, ("x", "zhh", "zhl")).reshape(16, 128, 128)
    near = [
        swap(away, "zl"),
        swap(home, "ylo"),
        lax.ppermute(away, ("ylo", "zl"), [(0, 3), (1, 2), (2, 1), (3, 0)]),
    ]
    both, near, packed = lax.optimization_barrier((both, near, packed))
    both_co = swap(both, "co")
    weights = lax.all_gather(packed, CTX, axis=0, tiled=True).reshape(8, 2, 256, 512)
    near_co = [swap(part, "co") for part in near]

    sent = pl.pallas_call(
        attend,
        out_shape=jax.ShapeDtypeStruct((4, 528, 128), BF),
        in_specs=[SM] + [VM] * 6,
        out_specs=VM,
        compiler_params=pltpu.CompilerParams(vmem_limit_bytes=32 << 20),
        name="attend",
    )(spots, home, *near, both, both_co)
    came = exchange(sent.reshape(4 * 528, 128), ("ylo", "zl")).reshape(4, 528, 128)
    head_part = pl.pallas_call(
        project,
        out_shape=jax.ShapeDtypeStruct((128, 2048), BF),
        in_specs=[SM] + [VM] * 9,
        out_specs=VM,
        scratch_shapes=[pltpu.VMEM((4, 128, 128), BF)],
        compiler_params=pltpu.CompilerParams(vmem_limit_bytes=32 << 20),
        name="project",
    )(spots, came, home, *near, rest, *near_co)

    parts = exchange(head_part, "yhi").reshape(4, 32, 2048)
    attention_sum = jnp.sum(parts.astype(F32), axis=0)
    hidden_mine = features(lax.dynamic_slice(hidden, (32 * y, 0), (32, 4096)), zl)
    residual = (hidden_mine.astype(F32) + attention_sum).astype(BF)
    spread = jnp.broadcast_to(residual[None], (8, 32, 2048)).reshape(256, 2048)
    residual = exchange(spread, Y)
    residual_out = lax.dynamic_slice(residual, (0, 256 * y), (256, 256))

    gain = features(norm_gain[None], zl)
    keep, sent = pl.pallas_call(
        mix,
        out_shape=(
            jax.ShapeDtypeStruct((256, 640), F32),
            jax.ShapeDtypeStruct((256, 640), BF),
        ),
        in_specs=[SM] + [VM] * 3,
        out_specs=(VM, VM),
        compiler_params=pltpu.CompilerParams(vmem_limit_bytes=32 << 20),
        name="mix",
    )(spots, residual, gain, weights)
    came = swap(sent, "zl").astype(F32)
    fine = (came[:, 528:533] + came[:, 520:525]) + came[:, 512:517]
    fine = keep[:, 512:517] + fine
    norm = lax.rsqrt(fine[:, 4:5] / 4096.0 + 1e-05)
    sum_x = (keep[:, :256] + came[:, :256]) * norm
    sum_bc = (keep[:, 256:512] + came[:, 256:512]) * norm
    sum_dt = fine[:, :4] * norm

    half = 128
    inputs_low = sum_x.astype(BF).reshape(2, half, 1, 4, 64)
    inputs = inputs_low.astype(F32)
    bc_round = sum_bc.astype(BF).reshape(2, half, 1, 256)
    b_low = bc_round[..., :128]
    c_low = bc_round[..., 128:]
    steps = jax.nn.softplus(sum_dt + dt_bias).reshape(2, half, 1, 4)
    rates = -jnp.exp(decay_log).reshape(1, 4)
    cumul = jnp.transpose(jnp.cumsum(steps * rates, axis=1), (0, 2, 3, 1))
    step_rows = jnp.transpose(steps, (0, 2, 3, 1))
    gram = jnp.einsum("ckgn,csgn->cgks", c_low, b_low, preferred_element_type=F32)
    places = jnp.arange(half, dtype=jnp.int32)
    causal = places[None, :] <= places[:, None]
    gaps = cumul[..., :, None] - cumul[..., None, :]
    decay = jnp.where(causal, jnp.exp(jnp.where(causal, gaps, 0.0)), 0.0)
    mixing = gram[:, :, None] * decay * step_rows[..., None, :]
    inner = split_product("cgjks,csgjp->ckgjp", mixing, inputs_low)
    last = cumul[..., -1]
    tail = jnp.exp(last[..., None] - cumul) * step_rows
    weighted = jnp.transpose(tail, (0, 3, 1, 2))[..., None] * inputs
    block_state = split_product("csgjp,csgn->cgjpn", weighted, b_low)
    block_decay = jnp.exp(last)

    rows = jnp.transpose(block_state.astype(BF).reshape(2, 32, 8, 128), (1, 0, 2, 3)).reshape(32, 16, 128)
    decays = jnp.repeat(jnp.concatenate(split3(block_decay.reshape(2, 4))).T, 8, axis=0)
    decays = jnp.broadcast_to(decays[..., None], (32, 6, 128))
    sent = jnp.concatenate([rows, decays, jnp.zeros((32, 10, 128), BF)], axis=1)
    came = exchange(sent, CTX)
    entering = pl.pallas_call(
        scan,
        out_shape=jax.ShapeDtypeStruct((32, 16, 128), BF),
        in_specs=[VM],
        out_specs=VM,
        name="scan",
    )(came)
    entering = exchange(entering, CTX)
    entering = jnp.transpose(entering.reshape(32, 2, 8, 128), (1, 0, 2, 3)).reshape(2, 1, 4, 64, 128)

    carried = jnp.transpose(jnp.exp(cumul), (0, 3, 1, 2))[..., None] * jnp.einsum(
        "cgjpn,ckgn->ckgjp", entering, c_low, preferred_element_type=F32
    )
    output = inner + carried + skip_gain.reshape(1, 4)[:, :, None] * inputs
    mamba_out = output.reshape(256, 256).astype(BF)
    return (residual_out, mamba_out)


def solution(mesh):
    fine = Mesh(mesh.devices.reshape(SIZES), AXES)
    placed = (
        P(CTX, TP),
        P(CTX, None, None),
        P(CTX, None, None),
        P(CTX, None),
        P(TP, None),
        P(),
        P(CTX, TP),
        P(CTX, None, None),
        P(CTX, TP),
        P(TP),
        P(TP),
        P(TP),
    )
    return jax.shard_map(
        body,
        mesh=fine,
        in_specs=placed,
        out_specs=(P(CTX, TP), P(CTX, TP)),
        check_vma=False,
    )
```

```python
import functools
import math

import jax
import jax.numpy as jnp
from jax import lax
from jax.experimental import pallas as pl
from jax.experimental.pallas import tpu as pltpu
from jax.sharding import Mesh
from jax.sharding import PartitionSpec as P

AXES = ("x", "zhh", "zhl", "co", "yhi", "ylo", "zl")
SIZES = (4, 2, 2, 2, 4, 2, 2)
ZH = ("zhh", "zhl")
CTX = ("x", "zhh", "zhl", "co")
Y = ("yhi", "ylo")
TP = ("yhi", "ylo", "zl")
BF = jnp.bfloat16
F32 = jnp.float32
LOWEST = -1e30


def split3(value):
    first = value.astype(BF)
    rest = value - first.astype(F32)
    second = rest.astype(BF)
    third = (rest - second.astype(F32)).astype(BF)
    return first, second, third


def split3_kept(value):
    first = lax.reduce_precision(value, 8, 7)
    rest = value - first
    second = lax.reduce_precision(rest, 8, 7)
    third = rest - second
    return first.astype(BF), second.astype(BF), third.astype(BF)


def features(value, zl):
    return jnp.concatenate(
        [
            lax.dynamic_slice_in_dim(value, 512 * i + 256 * zl, 256, 1)
            for i in range(8)
        ],
        axis=1,
    )


def swap(value, axis):
    return lax.ppermute(value, axis, [(0, 1), (1, 0)])


def exchange(value, axes):
    return lax.all_to_all(value, axes, split_axis=0, concat_axis=0, tiled=True)


def split_product(form, wide, narrow):
    upper = wide.astype(BF)
    lower = (wide - upper.astype(F32)).astype(BF)
    first_term = jnp.einsum(form, upper, narrow, preferred_element_type=F32)
    return first_term + jnp.einsum(form, lower, narrow, preferred_element_type=F32)


def pick(spots, q_ref, w_hbm, home_ref, away_ref, rest_ref, sems):
    zl, co = spots[2], spots[3]
    copies = []
    for at, (out_ref, side, half) in enumerate(
        ((home_ref, zl, co), (away_ref, 1 - zl, co), (rest_ref, zl, 1 - co))
    ):
        for i in range(4):
            start = pl.multiple_of(2048 * half + 512 * i + 256 * side, 256)
            copies.append(
                pltpu.make_async_copy(
                    w_hbm.at[:, pl.ds(start, 256)],
                    out_ref.at[:128, 256 * i : 256 * (i + 1)],
                    sems.at[4 * at + i],
                )
            )
    for copy in copies:
        copy.start()
    for i in range(8):
        block = q_ref[32 * i : 32 * (i + 1)]
        home_ref[128:, 128 * i : 128 * (i + 1)] = block
        away_ref[128:, 128 * i : 128 * (i + 1)] = block
    for copy in copies:
        copy.wait()


def attend(first, spots, home_ref, zl_ref, ylo_ref, both_ref, kv_ref, *refs):
    ctx, quarter, co = spots[0], spots[1], spots[3]
    core = co if first else 1 - co
    if first:
        sums_ref, stats_ref = refs
    else:
        sums_ref, stats_ref, out_ref = refs
    lane = lax.broadcasted_iota(jnp.int32, (32, 128), 1)
    token = lane % 64 // 32 * 64 + lane // 64 * 32 + lane % 32
    reach = token - lax.broadcasted_iota(jnp.int32, (32, 128), 0) - 32 * quarter
    first_reach = reach + 128 * ctx
    second_reach = reach + 128 * (63 - ctx)

    def rows(chunk, start):
        return jnp.concatenate(
            [kv_ref[8 * chunk + i, start : start + 32] for i in range(8)]
        )

    def peak(tiles):
        top = tiles[0]
        for tile in tiles[1:]:
            top = jnp.maximum(top, tile)
        return jnp.max(top, axis=0, keepdims=True)

    levels = []
    for head in range(4):
        q_ref = (home_ref, zl_ref, ylo_ref, both_ref)[head]
        query = jnp.concatenate(
            [
                q_ref[128:, 128 * i : 128 * (i + 1)]
                for i in (0, 2, 1, 3, 4, 6, 5, 7)
            ]
        )
        early, full, late = [], [], []
        for chunk in range(2):
            scores, later = [
                lax.dot_general(
                    rows(chunk, start),
                    some,
                    (((1,), (1,)), ((), ())),
                    preferred_element_type=F32,
                )
                * (math.log2(math.e) / math.sqrt(128))
                for start, some in ((0, query), (32, query[128:]))
            ]
            for piece in range(8):
                at = slice(32 * piece, 32 * (piece + 1))
                block = (8 * chunk + piece) * 2 + core
                early.append(
                    jnp.where(first_reach >= block * 128, scores[at, :128], LOWEST)
                )
                full.append(scores[at, 128:])
                late.append(
                    jnp.where(second_reach >= (63 - block) * 128, later[at], LOWEST)
                )
        tops = [peak(early), jnp.maximum(peak(full), peak(late))]
        if not first:
            before = [stats_ref[head, i : i + 1] for i in range(4)]
            tops = [jnp.maximum(tops[i], before[i]) for i in range(2)]
            scales = [jnp.exp2(before[i] - tops[i]) for i in range(2)]
        totals = [jnp.zeros((32, 128), F32), jnp.zeros((32, 128), F32)]
        summed = jnp.zeros((128, 256), F32)
        added = jnp.zeros((128, 128), F32)
        for chunk in range(2):
            raised = [[], [], []]
            for piece in range(8 * chunk, 8 * chunk + 8):
                for i, (tiles, half) in enumerate(((early, 0), (full, 1), (late, 1))):
                    part = jnp.exp2(tiles[piece] - tops[half])
                    totals[half] = totals[half] + part
                    raised[i].append(part)
            raised = [jnp.concatenate(parts).astype(BF) for parts in raised]
            summed = summed + lax.dot_general(
                rows(chunk, 64),
                jnp.concatenate(raised[:2], axis=1),
                (((0,), (0,)), ((), ())),
                preferred_element_type=F32,
            )
            added = added + lax.dot_general(
                rows(chunk, 96), raised[2], (((0,), (0,)), ((), ())), preferred_element_type=F32
            )
        totals = [jnp.sum(total, axis=0, keepdims=True) for total in totals]
        summed = [summed[:, :128], summed[:, 128:] + added]
        if first:
            sums_ref[head, :, :128] = summed[0]
            sums_ref[head, :, 128:] = summed[1]
            stats_ref[head] = jnp.concatenate([*tops, *totals, jnp.zeros((4, 128), F32)])
            continue
        totals = [totals[i] + scales[i] * before[2 + i] for i in range(2)]
        share = [
            (
                (summed[i] + scales[i] * sums_ref[head, :, 128 * i : 128 * (i + 1)])
                / totals[i]
            ).astype(BF)
            for i in range(2)
        ]
        for dest in range(4):
            at = slice(64 * (dest // 2), 64 * (dest // 2) + 64)
            out_ref[dest, 128 * head : 128 * (head + 1)] = jnp.concatenate(
                [part[:, at] for part in share], axis=1
            )
        levels.append(
            [
                jnp.where(top > 0.5 * LOWEST, top + jnp.log2(total), LOWEST)
                for top, total in zip(tops, totals)
            ]
        )
    if first:
        return
    for dest in range(4):
        at = slice(64 * (dest // 2), 64 * (dest // 2) + 64)
        level = jnp.concatenate(
            [jnp.concatenate([part[:, at] for part in pair], axis=1) for pair in levels]
        )
        out_ref[dest, 512:528] = jnp.concatenate([*split3(level), jnp.zeros((4, 128), BF)])


def project(spots, came_ref, *refs):
    quarter, co = spots[1], spots[3]
    own_refs, rest_refs, out_ref, attended = refs[:4], refs[4:8], refs[8], refs[9]
    fine = [came_ref[source, 512:528].astype(F32) for source in range(4)]
    levels = [(part[8:12] + part[4:8]) + part[0:4] for part in fine]
    for head in range(4):
        level = [levels[s][head ^ s : (head ^ s) + 1] for s in range(4)]
        top = jnp.maximum(jnp.maximum(level[0], level[1]), jnp.maximum(level[2], level[3]))
        scales = [jnp.exp2(one - top) for one in level]
        total = (scales[0] + scales[1]) + (scales[2] + scales[3])
        joined = jnp.zeros((128, 128), F32)
        for source in range(4):
            slot = 128 * (head ^ source)
            joined = joined + (scales[source] / total) * came_ref[
                source, slot : slot + 128
            ].astype(F32)
        attended[head] = joined.astype(BF)
    four = jnp.concatenate([attended[quarter ^ r] for r in range(4)])

    def times(w_refs):
        rows = jnp.concatenate([w_ref[:128] for w_ref in w_refs])
        return lax.dot_general(
            four, rows, (((0,), (0,)), ((), ())), preferred_element_type=F32
        ).astype(BF)

    out_ref[:, pl.ds(pl.multiple_of(1024 * co, 1024), 1024)] = times(own_refs)
    out_ref[:, pl.ds(pl.multiple_of(1024 * (1 - co), 1024), 1024)] = times(rest_refs)


def mix(spots, r_ref, gain_ref, w_ref, keep_ref, sent_ref):
    zl = spots[2]
    value = r_ref[...].astype(F32)
    square = jnp.sum(value * value, axis=1, keepdims=True)
    gained = (value * gain_ref[...]).astype(BF)

    def times(side):
        total = None
        for p in range(8):
            product = jnp.dot(
                gained[:, 256 * p : 256 * (p + 1)],
                w_ref[p, side],
                preferred_element_type=F32,
            )
            total = product if total is None else total + product
        return total

    sums = [times(0), times(1)]
    lane = lax.broadcasted_iota(jnp.int32, (256, 128), 1)
    for mine in range(2):
        one = jnp.where(zl == mine, sums[0], sums[1])
        bc = jnp.concatenate([sums[0][:, 256:384], sums[1][:, 256:384]], axis=1)
        fine = jnp.where(lane == 4, square, one[:, 384:])
        if mine == 0:
            keep_ref[:, :256] = one[:, :256]
            keep_ref[:, 256:512] = bc
            keep_ref[:, 512:] = fine
        else:
            first, second, third = [part.astype(F32) for part in split3(fine)]
            fine = first + pltpu.roll(second, 8, 1) + pltpu.roll(third, 16, 1)
            sent_ref[:, :256] = one[:, :256].astype(BF)
            sent_ref[:, 256:512] = bc.astype(BF)
            sent_ref[:, 512:] = fine.astype(BF)


def scan(came_ref, out_ref):
    state = jnp.zeros((8, 128), F32)
    fine = [came_ref[i, 16:32].astype(F32) for i in range(32)]
    rows = [came_ref[i, :16].astype(F32) for i in range(32)]
    entering = []
    for i in range(32):
        entering.append(state)
        decay = (fine[i][4:5] + fine[i][2:3]) + fine[i][0:1]
        state = decay * state + rows[i][:8]
    for i in range(31, -1, -1):
        out_ref[i] = jnp.concatenate([entering[i], state]).astype(BF)
        decay = (fine[i][5:6] + fine[i][3:4]) + fine[i][1:2]
        state = decay * state + rows[i][8:]


VM = pl.BlockSpec(memory_space=pltpu.VMEM)
SM = pl.BlockSpec(memory_space=pltpu.SMEM)
HB = pl.BlockSpec(memory_space=pl.ANY)


def body(
    queries,
    key_heads,
    head_values,
    hidden,
    out_proj,
    norm_gain,
    x_proj,
    bc_proj,
    dt_proj,
    dt_bias,
    decay_log,
    skip_gain,
):
    ctx = lax.axis_index(CTX)
    group = lax.axis_index("yhi")
    ylo = lax.axis_index("ylo")
    zl = lax.axis_index("zl")
    y = lax.axis_index(Y)
    quarter = 2 * ylo + zl

    bc_half = lax.dynamic_slice(bc_proj, (0, group, 128 * zl), (128, 1, 128))[:, 0]
    packed = jnp.concatenate(
        [x_proj, bc_half, jnp.pad(dt_proj, ((0, 0), (0, 124)))], axis=1
    )
    packed = lax.ppermute(packed, ("zhl", "zl"), [(0, 0), (1, 2), (2, 1), (3, 3)])
    spots = jnp.stack([ctx, quarter, zl, lax.axis_index("co")]).astype(jnp.int32)

    home, away, rest = pl.pallas_call(
        pick,
        out_shape=(
            jax.ShapeDtypeStruct((160, 1024), BF),
            jax.ShapeDtypeStruct((160, 1024), BF),
            jax.ShapeDtypeStruct((128, 1024), BF),
        ),
        in_specs=[SM, VM, HB],
        out_specs=(VM, VM, VM),
        scratch_shapes=[pltpu.SemaphoreType.DMA((12,))],
        name="pick",
    )(spots, queries, out_proj)

    def part(heads):
        return lax.dynamic_slice(
            heads.reshape(2, 128, 4, 128), (0, 32 * quarter, group, 0), (2, 32, 1, 128)
        ).reshape(64, 128)

    both = jnp.concatenate([part(key_heads), part(head_values)])
    both = jnp.broadcast_to(both, (16, 128, 128)).reshape(2048, 128)
    both = exchange(both, ("x", "zhh", "zhl")).reshape(16, 128, 128)
    near = [
        swap(away, "zl"),
        swap(home, "ylo"),
        lax.ppermute(away, ("ylo", "zl"), [(0, 3), (1, 2), (2, 1), (3, 0)]),
    ]
    both, near, packed = lax.optimization_barrier((both, near, packed))
    both_co = swap(both, "co")
    weights = lax.all_gather(packed, CTX, axis=0, tiled=True).reshape(8, 2, 256, 512)
    near_co = [swap(part, "co") for part in near]

    so_far = pl.pallas_call(
        functools.partial(attend, True),
        out_shape=(
            jax.ShapeDtypeStruct((4, 128, 256), F32),
            jax.ShapeDtypeStruct((4, 8, 128), F32),
        ),
        in_specs=[SM] + [VM] * 5,
        out_specs=(VM, VM),
        compiler_params=pltpu.CompilerParams(vmem_limit_bytes=32 << 20),
        name="attend_own",
    )(spots, home, *near, both)
    sent = pl.pallas_call(
        functools.partial(attend, False),
        out_shape=jax.ShapeDtypeStruct((4, 528, 128), BF),
        in_specs=[SM] + [VM] * 7,
        out_specs=VM,
        compiler_params=pltpu.CompilerParams(vmem_limit_bytes=32 << 20),
        name="attend_other",
    )(spots, home, *near, both_co, *so_far)
    came = exchange(sent.reshape(4 * 528, 128), ("ylo", "zl")).reshape(4, 528, 128)
    head_part = pl.pallas_call(
        project,
        out_shape=jax.ShapeDtypeStruct((128, 2048), BF),
        in_specs=[SM] + [VM] * 9,
        out_specs=VM,
        scratch_shapes=[pltpu.VMEM((4, 128, 128), BF)],
        compiler_params=pltpu.CompilerParams(vmem_limit_bytes=32 << 20),
        name="project",
    )(spots, came, home, *near, rest, *near_co)

    parts = exchange(head_part, "yhi").reshape(4, 32, 2048)
    attention_sum = jnp.sum(parts.astype(F32), axis=0)
    hidden_mine = features(lax.dynamic_slice(hidden, (32 * y, 0), (32, 4096)), zl)
    residual = (hidden_mine.astype(F32) + attention_sum).astype(BF)
    spread = jnp.broadcast_to(residual[None], (8, 32, 2048)).reshape(256, 2048)
    residual = exchange(spread, Y)
    residual_out = lax.dynamic_slice(residual, (0, 256 * y), (256, 256))

    gain = features(norm_gain[None], zl)
    keep, sent = pl.pallas_call(
        mix,
        out_shape=(
            jax.ShapeDtypeStruct((256, 640), F32),
            jax.ShapeDtypeStruct((256, 640), BF),
        ),
        in_specs=[SM] + [VM] * 3,
        out_specs=(VM, VM),
        compiler_params=pltpu.CompilerParams(vmem_limit_bytes=32 << 20),
        name="mix",
    )(spots, residual, gain, weights)
    came = swap(sent, "zl").astype(F32)
    fine = (came[:, 528:533] + came[:, 520:525]) + came[:, 512:517]
    fine = keep[:, 512:517] + fine
    norm = lax.rsqrt(fine[:, 4:5] / 4096.0 + 1e-05)
    sum_x = (keep[:, :256] + came[:, :256]) * norm
    sum_bc = (keep[:, 256:512] + came[:, 256:512]) * norm
    sum_dt = fine[:, :4] * norm

    half = 128
    inputs_low = sum_x.astype(BF).reshape(2, half, 1, 4, 64)
    inputs = inputs_low.astype(F32)
    bc_round = sum_bc.astype(BF).reshape(2, half, 1, 256)
    b_low = bc_round[..., :128]
    c_low = bc_round[..., 128:]
    steps = jax.nn.softplus(sum_dt + dt_bias).reshape(2, half, 1, 4)
    rates = -jnp.exp(decay_log).reshape(1, 4)
    cumul = jnp.transpose(jnp.cumsum(steps * rates, axis=1), (0, 2, 3, 1))
    step_rows = jnp.transpose(steps, (0, 2, 3, 1))
    gram = jnp.einsum("ckgn,csgn->cgks", c_low, b_low, preferred_element_type=F32)
    places = jnp.arange(half, dtype=jnp.int32)
    causal = places[None, :] <= places[:, None]
    gaps = cumul[..., :, None] - cumul[..., None, :]
    decay = jnp.where(causal, jnp.exp(jnp.where(causal, gaps, 0.0)), 0.0)
    mixing = gram[:, :, None] * decay * step_rows[..., None, :]
    inner = split_product("cgjks,csgjp->ckgjp", mixing, inputs_low)
    last = cumul[..., -1]
    tail = jnp.exp(last[..., None] - cumul) * step_rows
    weighted = jnp.transpose(tail, (0, 3, 1, 2))[..., None] * inputs
    block_state = split_product("csgjp,csgn->cgjpn", weighted, b_low)
    block_decay = jnp.exp(last)

    rows = jnp.transpose(block_state.astype(BF).reshape(2, 32, 8, 128), (1, 0, 2, 3)).reshape(32, 16, 128)
    decays = jnp.repeat(jnp.concatenate(split3_kept(block_decay.reshape(2, 4))).T, 8, axis=0)
    decays = jnp.broadcast_to(decays[..., None], (32, 6, 128))
    sent = jnp.concatenate([rows, decays, jnp.zeros((32, 10, 128), BF)], axis=1)
    came = exchange(sent, CTX)
    entering = pl.pallas_call(
        scan,
        out_shape=jax.ShapeDtypeStruct((32, 16, 128), BF),
        in_specs=[VM],
        out_specs=VM,
        name="scan",
    )(came)
    entering = exchange(entering, CTX)
    entering = jnp.transpose(entering.reshape(32, 2, 8, 128), (1, 0, 2, 3)).reshape(2, 1, 4, 64, 128)

    carried = jnp.transpose(jnp.exp(cumul), (0, 3, 1, 2))[..., None] * jnp.einsum(
        "cgjpn,ckgn->ckgjp", entering, c_low, preferred_element_type=F32
    )
    output = inner + carried + skip_gain.reshape(1, 4)[:, :, None] * inputs
    mamba_out = output.reshape(256, 256).astype(BF)
    return (residual_out, mamba_out)


def solution(mesh):
    fine = Mesh(mesh.devices.reshape(SIZES), AXES)
    placed = (
        P(CTX, TP),
        P(CTX, None, None),
        P(CTX, None, None),
        P(CTX, None),
        P(TP, None),
        P(),
        P(CTX, TP),
        P(CTX, None, None),
        P(CTX, TP),
        P(TP),
        P(TP),
        P(TP),
    )
    return jax.shard_map(
        body,
        mesh=fine,
        in_specs=placed,
        out_specs=(P(CTX, TP), P(CTX, TP)),
        check_vma=False,
    )
```

```python
import functools
import math

import jax
import jax.numpy as jnp
from jax import lax
from jax.experimental import pallas as pl
from jax.experimental.pallas import tpu as pltpu
from jax.sharding import Mesh
from jax.sharding import PartitionSpec as P

AXES = ("x", "zhh", "zhl", "co", "yhi", "ylo", "zl")
SIZES = (4, 2, 2, 2, 4, 2, 2)
ZH = ("zhh", "zhl")
CTX = ("x", "zhh", "zhl", "co")
Y = ("yhi", "ylo")
TP = ("yhi", "ylo", "zl")
BF = jnp.bfloat16
F32 = jnp.float32
LOWEST = -1e30


def split3(value):
    first = value.astype(BF)
    rest = value - first.astype(F32)
    second = rest.astype(BF)
    third = (rest - second.astype(F32)).astype(BF)
    return first, second, third


def split3_kept(value):
    first = lax.reduce_precision(value, 8, 7)
    rest = value - first
    second = lax.reduce_precision(rest, 8, 7)
    third = rest - second
    return first.astype(BF), second.astype(BF), third.astype(BF)


def features(value, zl):
    return jnp.concatenate(
        [
            lax.dynamic_slice_in_dim(value, 512 * i + 256 * zl, 256, 1)
            for i in range(8)
        ],
        axis=1,
    )


def swap(value, axis):
    return lax.ppermute(value, axis, [(0, 1), (1, 0)])


def exchange(value, axes):
    return lax.all_to_all(value, axes, split_axis=0, concat_axis=0, tiled=True)


def split_product(form, wide, narrow):
    upper = wide.astype(BF)
    lower = (wide - upper.astype(F32)).astype(BF)
    first_term = jnp.einsum(form, upper, narrow, preferred_element_type=F32)
    return first_term + jnp.einsum(form, lower, narrow, preferred_element_type=F32)


def pick(spots, q_ref, w_hbm, home_ref, away_ref, rest_ref, sems):
    zl, co = spots[2], spots[3]
    copies = []
    for at, (out_ref, side, half) in enumerate(
        ((home_ref, zl, co), (away_ref, 1 - zl, co), (rest_ref, zl, 1 - co))
    ):
        for i in range(4):
            start = pl.multiple_of(2048 * half + 512 * i + 256 * side, 256)
            copies.append(
                pltpu.make_async_copy(
                    w_hbm.at[:, pl.ds(start, 256)],
                    out_ref.at[:128, 256 * i : 256 * (i + 1)],
                    sems.at[4 * at + i],
                )
            )
    for copy in copies:
        copy.start()
    for i in range(8):
        block = q_ref[32 * i : 32 * (i + 1)]
        home_ref[128:, 128 * i : 128 * (i + 1)] = block
        away_ref[128:, 128 * i : 128 * (i + 1)] = block
    for copy in copies:
        copy.wait()


def attend(first, spots, home_ref, zl_ref, ylo_ref, both_ref, kv_ref, *refs):
    ctx, quarter, co = spots[0], spots[1], spots[3]
    core = co if first else 1 - co
    if first:
        sums_ref, stats_ref = refs
    else:
        sums_ref, stats_ref, out_ref = refs
    lane = lax.broadcasted_iota(jnp.int32, (32, 128), 1)
    token = lane % 64 // 32 * 64 + lane // 64 * 32 + lane % 32
    reach = token - lax.broadcasted_iota(jnp.int32, (32, 128), 0) - 32 * quarter
    first_reach = reach + 128 * ctx
    second_reach = reach + 128 * (63 - ctx)

    def rows(chunk, start):
        return jnp.concatenate(
            [kv_ref[8 * chunk + i, start : start + 32] for i in range(8)]
        )

    def peak(tiles):
        top = tiles[0]
        for tile in tiles[1:]:
            top = jnp.maximum(top, tile)
        return jnp.max(top, axis=0, keepdims=True)

    levels = []
    for head in range(4):
        q_ref = (home_ref, zl_ref, ylo_ref, both_ref)[head]
        query = jnp.concatenate(
            [
                q_ref[32 * i : 32 * (i + 1)]
                if head == 3
                else q_ref[128:, 128 * i : 128 * (i + 1)]
                for i in (0, 2, 1, 3, 4, 6, 5, 7)
            ]
        )
        early, full, late = [], [], []
        for chunk in range(2):
            scores, later = [
                lax.dot_general(
                    rows(chunk, start),
                    some,
                    (((1,), (1,)), ((), ())),
                    preferred_element_type=F32,
                )
                * (math.log2(math.e) / math.sqrt(128))
                for start, some in ((0, query), (32, query[128:]))
            ]
            for piece in range(8):
                at = slice(32 * piece, 32 * (piece + 1))
                block = (8 * chunk + piece) * 2 + core
                early.append(
                    jnp.where(first_reach >= block * 128, scores[at, :128], LOWEST)
                )
                full.append(scores[at, 128:])
                late.append(
                    jnp.where(second_reach >= (63 - block) * 128, later[at], LOWEST)
                )
        tops = [peak(early), jnp.maximum(peak(full), peak(late))]
        if not first:
            before = [stats_ref[head, i : i + 1] for i in range(4)]
            tops = [jnp.maximum(tops[i], before[i]) for i in range(2)]
            scales = [jnp.exp2(before[i] - tops[i]) for i in range(2)]
        totals = [jnp.zeros((32, 128), F32), jnp.zeros((32, 128), F32)]
        summed = jnp.zeros((128, 256), F32)
        added = jnp.zeros((128, 128), F32)
        for chunk in range(2):
            raised = [[], [], []]
            for piece in range(8 * chunk, 8 * chunk + 8):
                for i, (tiles, half) in enumerate(((early, 0), (full, 1), (late, 1))):
                    part = jnp.exp2(tiles[piece] - tops[half])
                    totals[half] = totals[half] + part
                    raised[i].append(part)
            raised = [jnp.concatenate(parts).astype(BF) for parts in raised]
            summed = summed + lax.dot_general(
                rows(chunk, 64),
                jnp.concatenate(raised[:2], axis=1),
                (((0,), (0,)), ((), ())),
                preferred_element_type=F32,
            )
            added = added + lax.dot_general(
                rows(chunk, 96), raised[2], (((0,), (0,)), ((), ())), preferred_element_type=F32
            )
        totals = [jnp.sum(total, axis=0, keepdims=True) for total in totals]
        summed = [summed[:, :128], summed[:, 128:] + added]
        if first:
            sums_ref[head, :, :128] = summed[0]
            sums_ref[head, :, 128:] = summed[1]
            stats_ref[head] = jnp.concatenate([*tops, *totals, jnp.zeros((4, 128), F32)])
            continue
        totals = [totals[i] + scales[i] * before[2 + i] for i in range(2)]
        share = [
            (
                (summed[i] + scales[i] * sums_ref[head, :, 128 * i : 128 * (i + 1)])
                / totals[i]
            ).astype(BF)
            for i in range(2)
        ]
        for dest in range(4):
            at = slice(64 * (dest // 2), 64 * (dest // 2) + 64)
            out_ref[dest, 128 * head : 128 * (head + 1)] = jnp.concatenate(
                [part[:, at] for part in share], axis=1
            )
        levels.append(
            [
                jnp.where(top > 0.5 * LOWEST, top + jnp.log2(total), LOWEST)
                for top, total in zip(tops, totals)
            ]
        )
    if first:
        return
    for dest in range(4):
        at = slice(64 * (dest // 2), 64 * (dest // 2) + 64)
        level = jnp.concatenate(
            [jnp.concatenate([part[:, at] for part in pair], axis=1) for pair in levels]
        )
        out_ref[dest, 512:528] = jnp.concatenate([*split3(level), jnp.zeros((4, 128), BF)])


def project(spots, came_ref, *refs):
    quarter, co = spots[1], spots[3]
    own_refs, rest_refs, out_ref, attended = refs[:4], refs[4:8], refs[8], refs[9]
    fine = [came_ref[source, 512:528].astype(F32) for source in range(4)]
    levels = [(part[8:12] + part[4:8]) + part[0:4] for part in fine]
    for head in range(4):
        level = [levels[s][head ^ s : (head ^ s) + 1] for s in range(4)]
        top = jnp.maximum(jnp.maximum(level[0], level[1]), jnp.maximum(level[2], level[3]))
        scales = [jnp.exp2(one - top) for one in level]
        total = (scales[0] + scales[1]) + (scales[2] + scales[3])
        joined = jnp.zeros((128, 128), F32)
        for source in range(4):
            slot = 128 * (head ^ source)
            joined = joined + (scales[source] / total) * came_ref[
                source, slot : slot + 128
            ].astype(F32)
        attended[head] = joined.astype(BF)
    four = jnp.concatenate([attended[quarter ^ r] for r in range(4)])

    def times(w_refs):
        rows = jnp.concatenate([w_ref[:128] for w_ref in w_refs])
        return lax.dot_general(
            four, rows, (((0,), (0,)), ((), ())), preferred_element_type=F32
        ).astype(BF)

    out_ref[:, pl.ds(pl.multiple_of(1024 * co, 1024), 1024)] = times(own_refs)
    out_ref[:, pl.ds(pl.multiple_of(1024 * (1 - co), 1024), 1024)] = times(rest_refs)


def mix(spots, r_ref, gain_ref, w_ref, keep_ref, sent_ref):
    zl = spots[2]
    value = r_ref[...].astype(F32)
    square = jnp.sum(value * value, axis=1, keepdims=True)
    gained = (value * gain_ref[...]).astype(BF)

    def times(side):
        total = None
        for p in range(8):
            product = jnp.dot(
                gained[:, 256 * p : 256 * (p + 1)],
                w_ref[p, side],
                preferred_element_type=F32,
            )
            total = product if total is None else total + product
        return total

    sums = [times(0), times(1)]
    lane = lax.broadcasted_iota(jnp.int32, (256, 128), 1)
    for mine in range(2):
        one = jnp.where(zl == mine, sums[0], sums[1])
        bc = jnp.concatenate([sums[0][:, 256:384], sums[1][:, 256:384]], axis=1)
        fine = jnp.where(lane == 4, square, one[:, 384:])
        if mine == 0:
            keep_ref[:, :256] = one[:, :256]
            keep_ref[:, 256:512] = bc
            keep_ref[:, 512:] = fine
        else:
            first, second, third = [part.astype(F32) for part in split3(fine)]
            fine = first + pltpu.roll(second, 8, 1) + pltpu.roll(third, 16, 1)
            sent_ref[:, :256] = one[:, :256].astype(BF)
            sent_ref[:, 256:512] = bc.astype(BF)
            sent_ref[:, 512:] = fine.astype(BF)


def scan(came_ref, out_ref):
    state = jnp.zeros((8, 128), F32)
    fine = [came_ref[i, 16:32].astype(F32) for i in range(32)]
    rows = [came_ref[i, :16].astype(F32) for i in range(32)]
    entering = []
    for i in range(32):
        entering.append(state)
        decay = (fine[i][4:5] + fine[i][2:3]) + fine[i][0:1]
        state = decay * state + rows[i][:8]
    for i in range(31, -1, -1):
        out_ref[i] = jnp.concatenate([entering[i], state]).astype(BF)
        decay = (fine[i][5:6] + fine[i][3:4]) + fine[i][1:2]
        state = decay * state + rows[i][8:]


VM = pl.BlockSpec(memory_space=pltpu.VMEM)
SM = pl.BlockSpec(memory_space=pltpu.SMEM)
HB = pl.BlockSpec(memory_space=pl.ANY)


def body(
    queries,
    key_heads,
    head_values,
    hidden,
    out_proj,
    norm_gain,
    x_proj,
    bc_proj,
    dt_proj,
    dt_bias,
    decay_log,
    skip_gain,
):
    ctx = lax.axis_index(CTX)
    group = lax.axis_index("yhi")
    ylo = lax.axis_index("ylo")
    zl = lax.axis_index("zl")
    y = lax.axis_index(Y)
    quarter = 2 * ylo + zl

    bc_half = lax.dynamic_slice(bc_proj, (0, group, 128 * zl), (128, 1, 128))[:, 0]
    packed = jnp.concatenate(
        [x_proj, bc_half, jnp.pad(dt_proj, ((0, 0), (0, 124)))], axis=1
    )
    packed = lax.ppermute(packed, ("zhl", "zl"), [(0, 0), (1, 2), (2, 1), (3, 3)])
    spots = jnp.stack([ctx, quarter, zl, lax.axis_index("co")]).astype(jnp.int32)

    home, away, rest = pl.pallas_call(
        pick,
        out_shape=(
            jax.ShapeDtypeStruct((160, 1024), BF),
            jax.ShapeDtypeStruct((160, 1024), BF),
            jax.ShapeDtypeStruct((128, 1024), BF),
        ),
        in_specs=[SM, VM, HB],
        out_specs=(VM, VM, VM),
        scratch_shapes=[pltpu.SemaphoreType.DMA((12,))],
        name="pick",
    )(spots, queries, out_proj)

    def part(heads):
        return lax.dynamic_slice(
            heads.reshape(2, 128, 4, 128), (0, 32 * quarter, group, 0), (2, 32, 1, 128)
        ).reshape(64, 128)

    both = jnp.concatenate([part(key_heads), part(head_values)])
    both = jnp.broadcast_to(both, (16, 128, 128)).reshape(2048, 128)
    both = exchange(both, ("x", "zhh", "zhl")).reshape(16, 128, 128)
    near = [
        swap(away, "zl"),
        swap(home, "ylo"),
        lax.ppermute(queries, ("ylo", "zl"), [(0, 3), (1, 2), (2, 1), (3, 0)]),
    ]
    both, near, packed = lax.optimization_barrier((both, near, packed))
    both_co = swap(both, "co")
    weights = lax.all_gather(packed, CTX, axis=0, tiled=True).reshape(8, 2, 256, 512)
    passed = swap(near[0], "ylo")

    so_far = pl.pallas_call(
        functools.partial(attend, True),
        out_shape=(
            jax.ShapeDtypeStruct((4, 128, 256), F32),
            jax.ShapeDtypeStruct((4, 8, 128), F32),
        ),
        in_specs=[SM] + [VM] * 5,
        out_specs=(VM, VM),
        compiler_params=pltpu.CompilerParams(vmem_limit_bytes=32 << 20),
        name="attend_own",
    )(spots, home, *near, both)
    sent = pl.pallas_call(
        functools.partial(attend, False),
        out_shape=jax.ShapeDtypeStruct((4, 528, 128), BF),
        in_specs=[SM] + [VM] * 7,
        out_specs=VM,
        compiler_params=pltpu.CompilerParams(vmem_limit_bytes=32 << 20),
        name="attend_other",
    )(spots, home, *near, both_co, *so_far)
    sent, passed = lax.optimization_barrier((sent, passed))
    rows = [near[0], near[1], passed]
    rows_co = [swap(part, "co") for part in rows]
    came = exchange(sent.reshape(4 * 528, 128), ("ylo", "zl")).reshape(4, 528, 128)
    head_part = pl.pallas_call(
        project,
        out_shape=jax.ShapeDtypeStruct((128, 2048), BF),
        in_specs=[SM] + [VM] * 9,
        out_specs=VM,
        scratch_shapes=[pltpu.VMEM((4, 128, 128), BF)],
        compiler_params=pltpu.CompilerParams(vmem_limit_bytes=32 << 20),
        name="project",
    )(spots, came, home, *rows, rest, *rows_co)

    parts = exchange(head_part, "yhi").reshape(4, 32, 2048)
    attention_sum = jnp.sum(parts.astype(F32), axis=0)
    hidden_mine = features(lax.dynamic_slice(hidden, (32 * y, 0), (32, 4096)), zl)
    residual = (hidden_mine.astype(F32) + attention_sum).astype(BF)
    spread = jnp.broadcast_to(residual[None], (8, 32, 2048)).reshape(256, 2048)
    residual = exchange(spread, Y)
    residual_out = lax.dynamic_slice(residual, (0, 256 * y), (256, 256))

    gain = features(norm_gain[None], zl)
    keep, sent = pl.pallas_call(
        mix,
        out_shape=(
            jax.ShapeDtypeStruct((256, 640), F32),
            jax.ShapeDtypeStruct((256, 640), BF),
        ),
        in_specs=[SM] + [VM] * 3,
        out_specs=(VM, VM),
        compiler_params=pltpu.CompilerParams(vmem_limit_bytes=32 << 20),
        name="mix",
    )(spots, residual, gain, weights)
    came = swap(sent, "zl").astype(F32)
    fine = (came[:, 528:533] + came[:, 520:525]) + came[:, 512:517]
    fine = keep[:, 512:517] + fine
    norm = lax.rsqrt(fine[:, 4:5] / 4096.0 + 1e-05)
    sum_x = (keep[:, :256] + came[:, :256]) * norm
    sum_bc = (keep[:, 256:512] + came[:, 256:512]) * norm
    sum_dt = fine[:, :4] * norm

    half = 128
    inputs_low = sum_x.astype(BF).reshape(2, half, 1, 4, 64)
    inputs = inputs_low.astype(F32)
    bc_round = sum_bc.astype(BF).reshape(2, half, 1, 256)
    b_low = bc_round[..., :128]
    c_low = bc_round[..., 128:]
    steps = jax.nn.softplus(sum_dt + dt_bias).reshape(2, half, 1, 4)
    rates = -jnp.exp(decay_log).reshape(1, 4)
    cumul = jnp.transpose(jnp.cumsum(steps * rates, axis=1), (0, 2, 3, 1))
    step_rows = jnp.transpose(steps, (0, 2, 3, 1))
    gram = jnp.einsum("ckgn,csgn->cgks", c_low, b_low, preferred_element_type=F32)
    places = jnp.arange(half, dtype=jnp.int32)
    causal = places[None, :] <= places[:, None]
    gaps = cumul[..., :, None] - cumul[..., None, :]
    decay = jnp.where(causal, jnp.exp(jnp.where(causal, gaps, 0.0)), 0.0)
    mixing = gram[:, :, None] * decay * step_rows[..., None, :]
    inner = split_product("cgjks,csgjp->ckgjp", mixing, inputs_low)
    last = cumul[..., -1]
    tail = jnp.exp(last[..., None] - cumul) * step_rows
    weighted = jnp.transpose(tail, (0, 3, 1, 2))[..., None] * inputs
    block_state = split_product("csgjp,csgn->cgjpn", weighted, b_low)
    block_decay = jnp.exp(last)

    rows = jnp.transpose(block_state.astype(BF).reshape(2, 32, 8, 128), (1, 0, 2, 3)).reshape(32, 16, 128)
    decays = jnp.repeat(jnp.concatenate(split3_kept(block_decay.reshape(2, 4))).T, 8, axis=0)
    decays = jnp.broadcast_to(decays[..., None], (32, 6, 128))
    sent = jnp.concatenate([rows, decays, jnp.zeros((32, 10, 128), BF)], axis=1)
    came = exchange(sent, CTX)
    entering = pl.pallas_call(
        scan,
        out_shape=jax.ShapeDtypeStruct((32, 16, 128), BF),
        in_specs=[VM],
        out_specs=VM,
        name="scan",
    )(came)
    entering = exchange(entering, CTX)
    entering = jnp.transpose(entering.reshape(32, 2, 8, 128), (1, 0, 2, 3)).reshape(2, 1, 4, 64, 128)

    carried = jnp.transpose(jnp.exp(cumul), (0, 3, 1, 2))[..., None] * jnp.einsum(
        "cgjpn,ckgn->ckgjp", entering, c_low, preferred_element_type=F32
    )
    output = inner + carried + skip_gain.reshape(1, 4)[:, :, None] * inputs
    mamba_out = output.reshape(256, 256).astype(BF)
    return (residual_out, mamba_out)


def solution(mesh):
    fine = Mesh(mesh.devices.reshape(SIZES), AXES)
    placed = (
        P(CTX, TP),
        P(CTX, None, None),
        P(CTX, None, None),
        P(CTX, None),
        P(TP, None),
        P(),
        P(CTX, TP),
        P(CTX, None, None),
        P(CTX, TP),
        P(TP),
        P(TP),
        P(TP),
    )
    return jax.shard_map(
        body,
        mesh=fine,
        in_specs=placed,
        out_specs=(P(CTX, TP), P(CTX, TP)),
        check_vma=False,
    )
```

```python
import functools
import math

import jax
import jax.numpy as jnp
from jax import lax
from jax.experimental import pallas as pl
from jax.experimental.pallas import tpu as pltpu
from jax.sharding import Mesh
from jax.sharding import PartitionSpec as P

AXES = ("x", "zhh", "zhl", "co", "yhi", "ylo", "zl")
SIZES = (4, 2, 2, 2, 4, 2, 2)
ZH = ("zhh", "zhl")
CTX = ("x", "zhh", "zhl", "co")
Y = ("yhi", "ylo")
TP = ("yhi", "ylo", "zl")
BF = jnp.bfloat16
F32 = jnp.float32
LOWEST = -1e30


def split3(value):
    first = value.astype(BF)
    rest = value - first.astype(F32)
    second = rest.astype(BF)
    third = (rest - second.astype(F32)).astype(BF)
    return first, second, third


def split3_kept(value):
    first = lax.reduce_precision(value, 8, 7)
    rest = value - first
    second = lax.reduce_precision(rest, 8, 7)
    third = rest - second
    return first.astype(BF), second.astype(BF), third.astype(BF)


def features(value, zl):
    return jnp.concatenate(
        [
            lax.dynamic_slice_in_dim(value, 512 * i + 256 * zl, 256, 1)
            for i in range(8)
        ],
        axis=1,
    )


def swap(value, axis):
    return lax.ppermute(value, axis, [(0, 1), (1, 0)])


def exchange(value, axes):
    return lax.all_to_all(value, axes, split_axis=0, concat_axis=0, tiled=True)


def split_product(form, wide, narrow):
    upper = wide.astype(BF)
    lower = (wide - upper.astype(F32)).astype(BF)
    first_term = jnp.einsum(form, upper, narrow, preferred_element_type=F32)
    return first_term + jnp.einsum(form, lower, narrow, preferred_element_type=F32)


def pick(spots, q_ref, w_hbm, home_ref, away_ref, rest_ref, sems):
    zl, co = spots[2], spots[3]
    copies = []
    for at, (out_ref, side, half) in enumerate(
        ((home_ref, zl, co), (away_ref, 1 - zl, co), (rest_ref, zl, 1 - co))
    ):
        for i in range(4):
            start = pl.multiple_of(2048 * half + 512 * i + 256 * side, 256)
            copies.append(
                pltpu.make_async_copy(
                    w_hbm.at[:, pl.ds(start, 256)],
                    out_ref.at[:128, 256 * i : 256 * (i + 1)],
                    sems.at[4 * at + i],
                )
            )
    for copy in copies:
        copy.start()
    for i in range(8):
        block = q_ref[32 * i : 32 * (i + 1)]
        home_ref[128:, 128 * i : 128 * (i + 1)] = block
        away_ref[128:, 128 * i : 128 * (i + 1)] = block
    for copy in copies:
        copy.wait()


def attend(first, spots, home_ref, zl_ref, ylo_ref, both_ref, kv_ref, *refs):
    ctx, quarter, co = spots[0], spots[1], spots[3]
    core = co if first else 1 - co
    if first:
        sums_ref, stats_ref = refs
    else:
        sums_ref, stats_ref, out_ref = refs
    lane = lax.broadcasted_iota(jnp.int32, (32, 128), 1)
    token = lane % 64 // 32 * 64 + lane // 64 * 32 + lane % 32
    reach = token - lax.broadcasted_iota(jnp.int32, (32, 128), 0) - 32 * quarter
    first_reach = reach + 128 * ctx
    second_reach = reach + 128 * (63 - ctx)

    def rows(chunk, start):
        return jnp.concatenate(
            [kv_ref[8 * chunk + i, start : start + 32] for i in range(8)]
        )

    def peak(tiles):
        top = tiles[0]
        for tile in tiles[1:]:
            top = jnp.maximum(top, tile)
        return jnp.max(top, axis=0, keepdims=True)

    levels = []
    for head in range(4):
        q_ref = (home_ref, zl_ref, ylo_ref, both_ref)[head]
        query = jnp.concatenate(
            [
                q_ref[32 * i : 32 * (i + 1)]
                if head == 3
                else q_ref[128:, 128 * i : 128 * (i + 1)]
                for i in (0, 2, 1, 3, 4, 6, 5, 7)
            ]
        )
        early, full, late = [], [], []
        for chunk in range(2):
            scores, later = [
                lax.dot_general(
                    rows(chunk, start),
                    some,
                    (((1,), (1,)), ((), ())),
                    preferred_element_type=F32,
                )
                * (math.log2(math.e) / math.sqrt(128))
                for start, some in ((0, query), (32, query[128:]))
            ]
            for piece in range(8):
                at = slice(32 * piece, 32 * (piece + 1))
                block = (8 * chunk + piece) * 2 + core
                early.append(
                    jnp.where(first_reach >= block * 128, scores[at, :128], LOWEST)
                )
                full.append(scores[at, 128:])
                late.append(
                    jnp.where(second_reach >= (63 - block) * 128, later[at], LOWEST)
                )
        tops = [peak(early), jnp.maximum(peak(full), peak(late))]
        if not first:
            before = [stats_ref[head, i : i + 1] for i in range(4)]
            tops = [jnp.maximum(tops[i], before[i]) for i in range(2)]
            scales = [jnp.exp2(before[i] - tops[i]) for i in range(2)]
        totals = [jnp.zeros((32, 128), F32), jnp.zeros((32, 128), F32)]
        summed = jnp.zeros((128, 256), F32)
        added = jnp.zeros((128, 128), F32)
        for chunk in range(2):
            raised = [[], [], []]
            for piece in range(8 * chunk, 8 * chunk + 8):
                for i, (tiles, half) in enumerate(((early, 0), (full, 1), (late, 1))):
                    part = jnp.exp2(tiles[piece] - tops[half])
                    totals[half] = totals[half] + part
                    raised[i].append(part)
            raised = [jnp.concatenate(parts).astype(BF) for parts in raised]
            summed = summed + lax.dot_general(
                rows(chunk, 64),
                jnp.concatenate(raised[:2], axis=1),
                (((0,), (0,)), ((), ())),
                preferred_element_type=F32,
            )
            added = added + lax.dot_general(
                rows(chunk, 96), raised[2], (((0,), (0,)), ((), ())), preferred_element_type=F32
            )
        totals = [jnp.sum(total, axis=0, keepdims=True) for total in totals]
        summed = [summed[:, :128], summed[:, 128:] + added]
        if first:
            sums_ref[head, :, :128] = summed[0]
            sums_ref[head, :, 128:] = summed[1]
            stats_ref[head] = jnp.concatenate([*tops, *totals, jnp.zeros((4, 128), F32)])
            continue
        totals = [totals[i] + scales[i] * before[2 + i] for i in range(2)]
        share = [
            (
                (summed[i] + scales[i] * sums_ref[head, :, 128 * i : 128 * (i + 1)])
                / totals[i]
            ).astype(BF)
            for i in range(2)
        ]
        for dest in range(4):
            at = slice(64 * (dest // 2), 64 * (dest // 2) + 64)
            out_ref[dest, 128 * head : 128 * (head + 1)] = jnp.concatenate(
                [part[:, at] for part in share], axis=1
            )
        levels.append(
            [
                jnp.where(top > 0.5 * LOWEST, top + jnp.log2(total), LOWEST)
                for top, total in zip(tops, totals)
            ]
        )
    if first:
        return
    for dest in range(4):
        at = slice(64 * (dest // 2), 64 * (dest // 2) + 64)
        level = jnp.concatenate(
            [jnp.concatenate([part[:, at] for part in pair], axis=1) for pair in levels]
        )
        out_ref[dest, 512:528] = jnp.concatenate([*split3(level), jnp.zeros((4, 128), BF)])


def project(spots, came_ref, *refs):
    quarter, co = spots[1], spots[3]
    own_refs, rest_refs, out_ref, attended = refs[:4], refs[4:8], refs[8], refs[9]
    fine = [came_ref[source, 512:528].astype(F32) for source in range(4)]
    levels = [(part[8:12] + part[4:8]) + part[0:4] for part in fine]
    for head in range(4):
        level = [levels[s][head ^ s : (head ^ s) + 1] for s in range(4)]
        top = jnp.maximum(jnp.maximum(level[0], level[1]), jnp.maximum(level[2], level[3]))
        scales = [jnp.exp2(one - top) for one in level]
        total = (scales[0] + scales[1]) + (scales[2] + scales[3])
        joined = jnp.zeros((128, 128), F32)
        for source in range(4):
            slot = 128 * (head ^ source)
            joined = joined + (scales[source] / total) * came_ref[
                source, slot : slot + 128
            ].astype(F32)
        attended[head] = joined.astype(BF)
    four = jnp.concatenate([attended[quarter ^ r] for r in range(4)])

    def times(w_refs):
        rows = jnp.concatenate([w_ref[:128] for w_ref in w_refs])
        return lax.dot_general(
            four, rows, (((0,), (0,)), ((), ())), preferred_element_type=F32
        ).astype(BF)

    out_ref[:, pl.ds(pl.multiple_of(1024 * co, 1024), 1024)] = times(own_refs)
    out_ref[:, pl.ds(pl.multiple_of(1024 * (1 - co), 1024), 1024)] = times(rest_refs)


def mix(spots, r_ref, gain_ref, w_ref, keep_ref, sent_ref):
    zl = spots[2]
    value = r_ref[...].astype(F32)
    square = jnp.sum(value * value, axis=1, keepdims=True)
    gained = (value * gain_ref[...]).astype(BF)

    def times(side):
        total = None
        for p in range(8):
            product = jnp.dot(
                gained[:, 256 * p : 256 * (p + 1)],
                w_ref[p, side],
                preferred_element_type=F32,
            )
            total = product if total is None else total + product
        return total

    sums = [times(0), times(1)]
    lane = lax.broadcasted_iota(jnp.int32, (256, 128), 1)
    for mine in range(2):
        one = jnp.where(zl == mine, sums[0], sums[1])
        bc = jnp.concatenate([sums[0][:, 256:384], sums[1][:, 256:384]], axis=1)
        fine = jnp.where(lane == 4, square, one[:, 384:])
        if mine == 0:
            keep_ref[:, :256] = one[:, :256]
            keep_ref[:, 256:512] = bc
            keep_ref[:, 512:] = fine
        else:
            first, second, third = [part.astype(F32) for part in split3(fine)]
            fine = first + pltpu.roll(second, 8, 1) + pltpu.roll(third, 16, 1)
            sent_ref[:, :256] = one[:, :256].astype(BF)
            sent_ref[:, 256:512] = bc.astype(BF)
            sent_ref[:, 512:] = fine.astype(BF)


def scan(came_ref, out_ref):
    state = jnp.zeros((8, 128), F32)
    fine = [came_ref[i, 16:32].astype(F32) for i in range(32)]
    rows = [came_ref[i, :16].astype(F32) for i in range(32)]
    entering = []
    for i in range(32):
        entering.append(state)
        decay = (fine[i][4:5] + fine[i][2:3]) + fine[i][0:1]
        state = decay * state + rows[i][:8]
    for i in range(31, -1, -1):
        out_ref[i] = jnp.concatenate([entering[i], state]).astype(BF)
        decay = (fine[i][5:6] + fine[i][3:4]) + fine[i][1:2]
        state = decay * state + rows[i][8:]


VM = pl.BlockSpec(memory_space=pltpu.VMEM)
SM = pl.BlockSpec(memory_space=pltpu.SMEM)
HB = pl.BlockSpec(memory_space=pl.ANY)


def body(
    queries,
    key_heads,
    head_values,
    hidden,
    out_proj,
    norm_gain,
    x_proj,
    bc_proj,
    dt_proj,
    dt_bias,
    decay_log,
    skip_gain,
):
    ctx = lax.axis_index(CTX)
    group = lax.axis_index("yhi")
    ylo = lax.axis_index("ylo")
    zl = lax.axis_index("zl")
    y = lax.axis_index(Y)
    quarter = 2 * ylo + zl

    bc_half = lax.dynamic_slice(bc_proj, (0, group, 128 * zl), (128, 1, 128))[:, 0]
    packed = jnp.concatenate(
        [x_proj, bc_half, jnp.pad(dt_proj, ((0, 0), (0, 124)))], axis=1
    )
    packed = lax.ppermute(packed, ("zhl", "zl"), [(0, 0), (1, 2), (2, 1), (3, 3)])
    spots = jnp.stack([ctx, quarter, zl, lax.axis_index("co")]).astype(jnp.int32)

    home, away, rest = pl.pallas_call(
        pick,
        out_shape=(
            jax.ShapeDtypeStruct((160, 1024), BF),
            jax.ShapeDtypeStruct((160, 1024), BF),
            jax.ShapeDtypeStruct((128, 1024), BF),
        ),
        in_specs=[SM, VM, HB],
        out_specs=(VM, VM, VM),
        scratch_shapes=[pltpu.SemaphoreType.DMA((12,))],
        name="pick",
    )(spots, queries, out_proj)

    def part(heads):
        return lax.dynamic_slice(
            heads.reshape(2, 128, 4, 128), (0, 32 * quarter, group, 0), (2, 32, 1, 128)
        ).reshape(64, 128)

    both = jnp.concatenate([part(key_heads), part(head_values)])
    both = jnp.broadcast_to(both, (16, 128, 128)).reshape(2048, 128)
    both = exchange(both, ("x", "zhh", "zhl")).reshape(16, 128, 128)
    near = [
        swap(away, "zl"),
        swap(home, "ylo"),
        lax.ppermute(queries, ("ylo", "zl"), [(0, 3), (1, 2), (2, 1), (3, 0)]),
    ]
    both, near, packed = lax.optimization_barrier((both, near, packed))
    both_co = swap(both, "co")
    weights = lax.all_gather(packed, CTX, axis=0, tiled=True).reshape(8, 2, 256, 512)
    passed = swap(near[0], "ylo")

    so_far = pl.pallas_call(
        functools.partial(attend, True),
        out_shape=(
            jax.ShapeDtypeStruct((4, 128, 256), F32),
            jax.ShapeDtypeStruct((4, 8, 128), F32),
        ),
        in_specs=[SM] + [VM] * 5,
        out_specs=(VM, VM),
        compiler_params=pltpu.CompilerParams(vmem_limit_bytes=32 << 20),
        name="attend_own",
    )(spots, home, *near, both)
    sent = pl.pallas_call(
        functools.partial(attend, False),
        out_shape=jax.ShapeDtypeStruct((4, 528, 128), BF),
        in_specs=[SM] + [VM] * 7,
        out_specs=VM,
        compiler_params=pltpu.CompilerParams(vmem_limit_bytes=32 << 20),
        name="attend_other",
    )(spots, home, *near, both_co, *so_far)
    sent, passed = lax.optimization_barrier((sent, passed))
    rows = [near[0], near[1], passed]
    rows_co = [swap(part, "co") for part in rows]
    came = exchange(sent.reshape(4 * 528, 128), ("ylo", "zl")).reshape(4, 528, 128)
    came, late_y = lax.optimization_barrier((came, y))
    head_part = pl.pallas_call(
        project,
        out_shape=jax.ShapeDtypeStruct((128, 2048), BF),
        in_specs=[SM] + [VM] * 9,
        out_specs=VM,
        scratch_shapes=[pltpu.VMEM((4, 128, 128), BF)],
        compiler_params=pltpu.CompilerParams(vmem_limit_bytes=32 << 20),
        name="project",
    )(spots, came, home, *rows, rest, *rows_co)

    parts = exchange(head_part, "yhi").reshape(4, 32, 2048)
    attention_sum = jnp.sum(parts.astype(F32), axis=0)
    hidden_mine = features(lax.dynamic_slice(hidden, (32 * late_y, 0), (32, 4096)), zl)
    residual = (hidden_mine.astype(F32) + attention_sum).astype(BF)
    spread = jnp.broadcast_to(residual[None], (8, 32, 2048)).reshape(256, 2048)
    residual = exchange(spread, Y)
    residual_out = lax.dynamic_slice(residual, (0, 256 * y), (256, 256))

    gain = features(norm_gain[None], zl)
    keep, sent = pl.pallas_call(
        mix,
        out_shape=(
            jax.ShapeDtypeStruct((256, 640), F32),
            jax.ShapeDtypeStruct((256, 640), BF),
        ),
        in_specs=[SM] + [VM] * 3,
        out_specs=(VM, VM),
        compiler_params=pltpu.CompilerParams(vmem_limit_bytes=32 << 20),
        name="mix",
    )(spots, residual, gain, weights)
    came = swap(sent, "zl").astype(F32)
    fine = (came[:, 528:533] + came[:, 520:525]) + came[:, 512:517]
    fine = keep[:, 512:517] + fine
    norm = lax.rsqrt(fine[:, 4:5] / 4096.0 + 1e-05)
    sum_x = (keep[:, :256] + came[:, :256]) * norm
    sum_bc = (keep[:, 256:512] + came[:, 256:512]) * norm
    sum_dt = fine[:, :4] * norm

    half = 128
    inputs_low = sum_x.astype(BF).reshape(2, half, 1, 4, 64)
    inputs = inputs_low.astype(F32)
    bc_round = sum_bc.astype(BF).reshape(2, half, 1, 256)
    b_low = bc_round[..., :128]
    c_low = bc_round[..., 128:]
    steps = jax.nn.softplus(sum_dt + dt_bias).reshape(2, half, 1, 4)
    rates = -jnp.exp(decay_log).reshape(1, 4)
    cumul = jnp.transpose(jnp.cumsum(steps * rates, axis=1), (0, 2, 3, 1))
    step_rows = jnp.transpose(steps, (0, 2, 3, 1))
    gram = jnp.einsum("ckgn,csgn->cgks", c_low, b_low, preferred_element_type=F32)
    places = jnp.arange(half, dtype=jnp.int32)
    causal = places[None, :] <= places[:, None]
    gaps = cumul[..., :, None] - cumul[..., None, :]
    decay = jnp.where(causal, jnp.exp(jnp.where(causal, gaps, 0.0)), 0.0)
    mixing = gram[:, :, None] * decay * step_rows[..., None, :]
    inner = split_product("cgjks,csgjp->ckgjp", mixing, inputs_low)
    last = cumul[..., -1]
    tail = jnp.exp(last[..., None] - cumul) * step_rows
    weighted = jnp.transpose(tail, (0, 3, 1, 2))[..., None] * inputs
    block_state = split_product("csgjp,csgn->cgjpn", weighted, b_low)
    block_decay = jnp.exp(last)

    rows = jnp.transpose(block_state.astype(BF).reshape(2, 32, 8, 128), (1, 0, 2, 3)).reshape(32, 16, 128)
    decays = jnp.repeat(jnp.concatenate(split3_kept(block_decay.reshape(2, 4))).T, 8, axis=0)
    decays = jnp.broadcast_to(decays[..., None], (32, 6, 128))
    sent = jnp.concatenate([rows, decays, jnp.zeros((32, 10, 128), BF)], axis=1)
    came = exchange(sent, CTX)
    entering = pl.pallas_call(
        scan,
        out_shape=jax.ShapeDtypeStruct((32, 16, 128), BF),
        in_specs=[VM],
        out_specs=VM,
        name="scan",
    )(came)
    entering = exchange(entering, CTX)
    entering = jnp.transpose(entering.reshape(32, 2, 8, 128), (1, 0, 2, 3)).reshape(2, 1, 4, 64, 128)

    carried = jnp.transpose(jnp.exp(cumul), (0, 3, 1, 2))[..., None] * jnp.einsum(
        "cgjpn,ckgn->ckgjp", entering, c_low, preferred_element_type=F32
    )
    output = inner + carried + skip_gain.reshape(1, 4)[:, :, None] * inputs
    mamba_out = output.reshape(256, 256).astype(BF)
    return (residual_out, mamba_out)


def solution(mesh):
    fine = Mesh(mesh.devices.reshape(SIZES), AXES)
    placed = (
        P(CTX, TP),
        P(CTX, None, None),
        P(CTX, None, None),
        P(CTX, None),
        P(TP, None),
        P(),
        P(CTX, TP),
        P(CTX, None, None),
        P(CTX, TP),
        P(TP),
        P(TP),
        P(TP),
    )
    return jax.shard_map(
        body,
        mesh=fine,
        in_specs=placed,
        out_specs=(P(CTX, TP), P(CTX, TP)),
        check_vma=False,
    )
```
